32 devices in a mesh: tower: 2 (over core), dp: 8 (over z, x), mp: 2 (over y).
Axes of the slice: x: 2, y: 2, z: 4, core: 2. Of those that a mesh axis runs over, the one named last changes fastest.
Arguments:
- tower_input: bfloat16 [2, 16, 256, 768], P('tower', 'dp'), may hold values from -6 to 6
- patch_order: int32 [16, 256], P('dp'), may hold values from 0 to 255, each once within a row
- visible_count: int32 [2, 16], P('tower', 'dp'), may hold values from 32 to 256, as said below
- joint_cotangent: bfloat16 [8, 2, 2, 1, 256, 768], P('dp', 'tower'), may hold values from -6 to 6
- mixer_in_copy: bfloat16 [2, 768, 3, 768], P('tower', None, None, 'mp'), may hold values from -0.21875 to 0.21875
- mixer_in_master: float32 [2, 768, 3, 768], P('tower', 'dp', None, 'mp'), may hold values from -0.21875 to 0.21875
- mixer_in_moment: float32 [2, 768, 3, 768], P('tower', 'dp', None, 'mp'), may hold values from -384 to 384
- mixer_in_average: float32 [2, 768, 3, 768], P('tower', 'dp', None, 'mp'), may hold values from -0.21875 to 0.21875
- mixer_out_copy: bfloat16 [2, 768, 768], P('tower', 'mp'), may hold values from -1.75 to 1.75
- mixer_out_master: float32 [2, 768, 768], P('tower', 'mp', 'dp'), may hold values from -1.75 to 1.75
- mixer_out_moment: float32 [2, 768, 768], P('tower', 'mp', 'dp'), may hold values from -32 to 32
- mixer_out_average: float32 [2, 768, 768], P('tower', 'mp', 'dp'), may hold values from -1.75 to 1.75
- expand_copy: bfloat16 [2, 768, 3072], P('tower', None, 'mp'), may hold values from -0.21875 to 0.21875
- expand_master: float32 [2, 768, 3072], P('tower', 'dp', 'mp'), may hold values from -0.21875 to 0.21875
- expand_moment: float32 [2, 768, 3072], P('tower', 'dp', 'mp'), may hold values from -80 to 80
- expand_average: float32 [2, 768, 3072], P('tower', 'dp', 'mp'), may hold values from -0.21875 to 0.21875
- contract_copy: bfloat16 [2, 3072, 768], P('tower', 'mp'), may hold values from -0.109375 to 0.109375
- contract_master: float32 [2, 3072, 768], P('tower', 'mp', 'dp'), may hold values from -0.109375 to 0.109375
- contract_moment: float32 [2, 3072, 768], P('tower', 'mp', 'dp'), may hold values from -160 to 160
- contract_average: float32 [2, 3072, 768], P('tower', 'mp', 'dp'), may hold values from -0.109375 to 0.109375
- norm_params_copy: bfloat16 [2, 4, 768], P('tower'), may hold values from -1.2 to 1.6
- norm_params_master: float32 [2, 4, 768], P('tower', None, 'dp'), may hold values from -1.2 to 1.6
- norm_params_moment: float32 [2, 4, 768], P('tower', None, 'dp'), may hold values from -512 to 512
- norm_params_average: float32 [2, 4, 768], P('tower', None, 'dp'), may hold values from -1.2 to 1.6
Outputs:
- joint_rows: bfloat16 [8, 2, 2, 1, 256, 768], P('dp', 'tower')
- input_grad: bfloat16 [2, 16, 256, 768], P('tower', 'dp')
- mixer_in_grad: float32 [2, 768, 3, 768], P('tower', 'dp', None, 'mp')
- mixer_in_master_new: float32 [2, 768, 3, 768], P('tower', 'dp', None, 'mp')
- mixer_in_moment_new: float32 [2, 768, 3, 768], P('tower', 'dp', None, 'mp')
- mixer_in_average_new: float32 [2, 768, 3, 768], P('tower', 'dp', None, 'mp')
- mixer_in_copy_new: bfloat16 [2, 768, 3, 768], P('tower', 'dp', None, 'mp')
- mixer_out_grad: float32 [2, 768, 768], P('tower', 'mp', 'dp')
- mixer_out_master_new: float32 [2, 768, 768], P('tower', 'mp', 'dp')
- mixer_out_moment_new: float32 [2, 768, 768], P('tower', 'mp', 'dp')
- mixer_out_average_new: float32 [2, 768, 768], P('tower', 'mp', 'dp')
- mixer_out_copy_new: bfloat16 [2, 768, 768], P('tower', 'mp', 'dp')
- expand_grad: float32 [2, 768, 3072], P('tower', 'dp', 'mp')
- expand_master_new: float32 [2, 768, 3072], P('tower', 'dp', 'mp')
- expand_moment_new: float32 [2, 768, 3072], P('tower', 'dp', 'mp')
- expand_average_new: float32 [2, 768, 3072], P('tower', 'dp', 'mp')
- expand_copy_new: bfloat16 [2, 768, 3072], P('tower', 'dp', 'mp')
- contract_grad: float32 [2, 3072, 768], P('tower', 'mp', 'dp')
- contract_master_new: float32 [2, 3072, 768], P('tower', 'mp', 'dp')
- contract_moment_new: float32 [2, 3072, 768], P('tower', 'mp', 'dp')
- contract_average_new: float32 [2, 3072, 768], P('tower', 'mp', 'dp')
- contract_copy_new: bfloat16 [2, 3072, 768], P('tower', 'mp', 'dp')
- norm_params_grad: float32 [2, 4, 768], P('tower', None, 'dp')
- norm_params_master_new: float32 [2, 4, 768], P('tower', None, 'dp')
- norm_params_moment_new: float32 [2, 4, 768], P('tower', None, 'dp')
- norm_params_average_new: float32 [2, 4, 768], P('tower', None, 'dp')
- norm_params_copy_new: bfloat16 [2, 4, 768], P('tower', None, 'dp')
The draws below stay inside these ranges and needn't reach their ends.
Inputs may be any that keep to these rules, and one draw needn't show every extreme that they name: `patch_order`: each row is a permutation of the 256 patches; the first visible_count[0, b] entries of row b are its visible patches. `visible_count`: in each of the two rows some entry equals 256.
All inputs are finite; a program needn't handle non-finite values.
Results may differ from the reference program's by a relative error of at most 0.015.
Values may be sent and summed in bfloat16 or wider, within the bound.
No kernel may reach another device: no remote copies, remote signals or barrier semaphores. Data moves between devices by JAX's collectives and lax.ppermute only.
A program may use at most 128 MiB of HBM per device.

```python
import math
import jax
import jax.numpy as jnp
from jax import lax

D = 768
HEADS = 12
HD = 64
FF = 3072
L = 256
SEQ_DEV = 2
SEQS = 16
N_DP = 8


def draw_visible_count(key, part):
    base = jax.random.randint(key, (2, SEQS), L // 8, L + 1)
    spot = jax.random.randint(jax.random.fold_in(key, 7), (2, 1), 0, SEQS)
    column = jnp.arange(SEQS, dtype=jnp.int32)[None, :]
    return jnp.where(column == spot, L, base).astype(jnp.int32)


def norm_law(key):
    noise = jnp.clip(jax.random.normal(key, (2, 4, D), jnp.float32), -6.0, 6.0)
    row_number = jnp.arange(4)[None, :, None]
    return jnp.where(row_number % 2 == 0, 1.0 + 0.1 * noise, 0.2 * noise)


def draw_norm_params_copy(key, part):
    return norm_law(jax.random.fold_in(key, 11)).astype(jnp.bfloat16)


def draw_norm_params_master(key, part):
    return norm_law(jax.random.fold_in(key, 12)).astype(jnp.float32)


def draw_norm_params_average(key, part):
    return norm_law(jax.random.fold_in(key, 13)).astype(jnp.float32)


def block_scale(rng, shape, cuts, least, top_value):
    level = 1.0
    for axis_at, blocks in cuts:
        draws = jax.random.uniform(jax.random.fold_in(jax.random.fold_in(rng, 6), axis_at), (blocks,), jnp.float32, least / len(cuts), top_value / len(cuts))
        level = level * jnp.repeat(jnp.exp(draws), shape[axis_at] // blocks).reshape((-1,) + (1,) * (len(shape) - 1 - axis_at))
    return level


def normal_values(rng, shape, width, bound, shards=(), kind=jnp.bfloat16):
    level = block_scale(rng, shape, shards, -0.22, 0.18) if shards else 1.0
    entries = jax.random.normal(rng, shape, jnp.float32) * width * level
    return jnp.minimum(jnp.maximum(entries, -bound), bound).astype(kind)


def setup_inputs(seed: int = 0) -> dict:
    key_list = jax.random.split(jax.random.key(seed), 25)
    return {
        "tower_input": normal_values(key_list[0], (2, SEQS, L, D), 1.0, 6.0, ((0, 2), (1, 8))),
        "patch_order": jax.vmap(lambda own: jax.random.permutation(own, L))(jax.random.split(key_list[1], SEQS)).reshape((SEQS, L)).astype(jnp.int32),
        "visible_count": draw_visible_count(jax.random.fold_in(key_list[24], 71), 0),
        "joint_cotangent": normal_values(key_list[3], (N_DP, 2, 2, SEQ_DEV // 2, L, D), 1.0, 6.0, ((0, 8), (1, 2))),
        "mixer_in_copy": normal_values(key_list[4], (2, D, 3, D), D ** -0.5, 0.21875, ((0, 2), (3, 2))),
        "mixer_in_master": normal_values(key_list[5], (2, D, 3, D), D ** -0.5, 0.21875, ((0, 2), (1, 8), (3, 2)), jnp.float32),
        "mixer_in_moment": normal_values(key_list[6], (2, D, 3, D), (1.0 * (SEQS * L) ** 0.5), 384.0, ((0, 2), (1, 8), (3, 2)), jnp.float32),
        "mixer_in_average": normal_values(key_list[7], (2, D, 3, D), D ** -0.5, 0.21875, ((0, 2), (1, 8), (3, 2)), jnp.float32),
        "mixer_out_copy": normal_values(key_list[8], (2, D, D), (D * 4 // L) ** -0.5, 1.75, ((0, 2), (1, 2))),
        "mixer_out_master": normal_values(key_list[9], (2, D, D), (D * 4 // L) ** -0.5, 1.75, ((0, 2), (1, 2), (2, 8)), jnp.float32),
        "mixer_out_moment": normal_values(key_list[10], (2, D, D), (0.08 * (SEQS * L) ** 0.5), 32.0, ((0, 2), (1, 2), (2, 8)), jnp.float32),
        "mixer_out_average": normal_values(key_list[11], (2, D, D), (D * 4 // L) ** -0.5, 1.75, ((0, 2), (1, 2), (2, 8)), jnp.float32),
        "expand_copy": normal_values(key_list[12], (2, D, FF), D ** -0.5, 0.21875, ((0, 2), (2, 2))),
        "expand_master": normal_values(key_list[13], (2, D, FF), D ** -0.5, 0.21875, ((0, 2), (1, 8), (2, 2)), jnp.float32),
        "expand_moment": normal_values(key_list[14], (2, D, FF), (0.22 * (SEQS * L) ** 0.5), 80.0, ((0, 2), (1, 8), (2, 2)), jnp.float32),
        "expand_average": normal_values(key_list[15], (2, D, FF), D ** -0.5, 0.21875, ((0, 2), (1, 8), (2, 2)), jnp.float32),
        "contract_copy": normal_values(key_list[16], (2, FF, D), FF ** -0.5, 0.109375, ((0, 2), (1, 2))),
        "contract_master": normal_values(key_list[17], (2, FF, D), FF ** -0.5, 0.109375, ((0, 2), (1, 2), (2, 8)), jnp.float32),
        "contract_moment": normal_values(key_list[18], (2, FF, D), (0.45 * (SEQS * L) ** 0.5), 160.0, ((0, 2), (1, 2), (2, 8)), jnp.float32),
        "contract_average": normal_values(key_list[19], (2, FF, D), FF ** -0.5, 0.109375, ((0, 2), (1, 2), (2, 8)), jnp.float32),
        "norm_params_copy": draw_norm_params_copy(jax.random.fold_in(key_list[24], 71), 0),
        "norm_params_master": draw_norm_params_master(jax.random.fold_in(key_list[24], 71), 0),
        "norm_params_moment": normal_values(key_list[22], (2, 4, D), (1.5 * (SEQS * L) ** 0.5), 512.0, ((0, 2), (2, 8)), jnp.float32),
        "norm_params_average": draw_norm_params_average(jax.random.fold_in(key_list[24], 71), 0),
    }


@jax.custom_vjp
def low(v):
    return lax.optimization_barrier(v.astype(jnp.bfloat16)).astype(jnp.float32)

@jax.custom_vjp
def low_back(v):
    return v

def low_keep(v):
    return (low(v), None)

def low_pass(kept, grad):
    return (grad,)

def back_keep(v):
    return (v, None)

def back_low(kept, grad):
    return (low(grad),)
low.defvjp(low_keep, low_pass)
low_back.defvjp(back_keep, back_low)
EPSILON = 1e-06
MOMENTUM = 0.9
AVERAGE_RATE = 0.6
STEP_RATES = (0.013, 1.3, 0.06, 0.015, 0.04)
HIGHEST = lax.Precision.HIGHEST

def normalize(layer_rows, gain_row, shift_row):
    centre = lax.optimization_barrier(jnp.mean(layer_rows, axis=-1, keepdims=True))
    spread = lax.optimization_barrier(jnp.mean(jnp.square(layer_rows - centre), axis=-1, keepdims=True))
    return (layer_rows - centre) * lax.rsqrt(spread + EPSILON) * gain_row + shift_row

def tower_layer(layer_rows, valid_mask, mixer_in, mixer_out, expand, contract, norm_params):
    group_size = layer_rows.shape[0]
    first_norm = low(normalize(layer_rows, norm_params[0], norm_params[1]))
    mixed_rows = low(low_back(jnp.einsum('bld,dce->blce', first_norm, mixer_in, precision=HIGHEST)))
    queries = mixed_rows[:, :, 0].reshape(group_size, L, HEADS, HD)
    key_rows = mixed_rows[:, :, 1].reshape(group_size, L, HEADS, HD)
    value_rows = mixed_rows[:, :, 2].reshape(group_size, L, HEADS, HD)
    scores = jnp.einsum('bqhd,bkhd->bhqk', queries, key_rows, precision=HIGHEST) * HD ** (-0.5)
    scores = low_back(scores)
    key_mask = valid_mask[:, None, None, :] > 0.5
    scores = jnp.where(key_mask, scores, -1e+30)
    row_top = lax.optimization_barrier(jnp.max(scores, axis=-1, keepdims=True))
    exponent = jnp.exp(scores - row_top)
    attention_probs = low(exponent / lax.optimization_barrier(jnp.sum(exponent, axis=-1, keepdims=True)))
    context = jnp.einsum('bhqk,bkhd->bqhd', attention_probs, value_rows, precision=HIGHEST).reshape(group_size, L, D)
    context = low(low_back(context))
    attended = low_back(jnp.einsum('bld,de->ble', context, mixer_out, precision=HIGHEST))
    middle = layer_rows + attended
    second_norm = low(normalize(middle, norm_params[2], norm_params[3]))
    pre_gelu = low_back(jnp.einsum('bld,df->blf', second_norm, expand, precision=HIGHEST))
    hidden = low(jax.nn.gelu(pre_gelu, approximate=False))
    output = low_back(jnp.einsum('blf,fd->bld', hidden, contract, precision=HIGHEST))
    return low((middle + output) * valid_mask[:, :, None])

def make_group_step(image_side, weights):

    def one_group(totals, piece):
        inputs_group, order_group, valid_group, returned_group = piece

        def forward(inputs_float, mixer_in, mixer_out, expand, contract, norm_params):
            if image_side:
                index_full = jnp.broadcast_to(order_group[:, :, None], inputs_float.shape)
                gathered = jnp.take_along_axis(inputs_float, index_full, axis=1)
            else:
                gathered = inputs_float
            return tower_layer(gathered * valid_group[:, :, None], valid_group, mixer_in, mixer_out, expand, contract, norm_params)
        final_rows, pullback = jax.vjp(forward, inputs_group, weights[0], weights[1], weights[2], weights[3], weights[4])
        gradients = pullback(returned_group)
        summed = tuple((total_part + new_part for total_part, new_part in zip(totals, gradients[1:])))
        return (summed, (final_rows, gradients[0]))
    return one_group

def reference(tower_input, patch_order, visible_count, joint_cotangent, mixer_in_copy, mixer_in_master, mixer_in_moment, mixer_in_average, mixer_out_copy, mixer_out_master, mixer_out_moment, mixer_out_average, expand_copy, expand_master, expand_moment, expand_average, contract_copy, contract_master, contract_moment, contract_average, norm_params_copy, norm_params_master, norm_params_moment, norm_params_average):
    copies = (mixer_in_copy, mixer_out_copy, expand_copy, contract_copy, norm_params_copy)
    masters = (mixer_in_master, mixer_out_master, expand_master, contract_master, norm_params_master)
    moments = (mixer_in_moment, mixer_out_moment, expand_moment, contract_moment, norm_params_moment)
    averages = (mixer_in_average, mixer_out_average, expand_average, contract_average, norm_params_average)
    group_size = 16
    while SEQS % group_size:
        group_size = group_size // 2
    group_count = SEQS // group_size
    slot_index = jnp.arange(L, dtype=jnp.int32)
    cotangent = joint_cotangent.astype(jnp.float32)
    final_all = []
    input_all = []
    grads_all = []
    for tower_index in range(2):
        weights = tuple((element[tower_index].astype(jnp.float32) for element in copies))
        valid_mask = (slot_index[None, :] < visible_count[tower_index][:, None]).astype(jnp.float32)
        inputs_here = tower_input[tower_index].astype(jnp.float32)
        returned = cotangent[:, :, tower_index].reshape(SEQS, L, D)
        if tower_index == 0:
            order_here = patch_order.astype(jnp.int32)
        else:
            order_here = jnp.broadcast_to(slot_index[None, :], (SEQS, L)).astype(jnp.int32)
        pieces = tuple((element.reshape((group_count, group_size) + element.shape[1:]) for element in (inputs_here, order_here, valid_mask, returned)))
        zero_init = tuple((jnp.zeros_like(element) for element in weights))
        totals, (finals, input_grads) = lax.scan(make_group_step(tower_index == 0, weights), zero_init, pieces)
        final_all.append(finals.reshape(N_DP, 2, SEQ_DEV // 2, L, D))
        input_all.append(input_grads.reshape(SEQS, L, D))
        grads_all.append(totals)
    joint_rows = jnp.stack(final_all, axis=2).astype(jnp.bfloat16)
    input_grad = jnp.stack(input_all, axis=0).astype(jnp.bfloat16)
    updates = []
    for param_index in range(5):
        gradient = jnp.stack([grads_all[0][param_index], grads_all[1][param_index]], axis=0)
        step_rate = STEP_RATES[param_index] / math.sqrt(SEQS * L)
        moment_new = MOMENTUM * moments[param_index] + gradient
        master_new = masters[param_index] - step_rate * (gradient + MOMENTUM * moment_new)
        average_new = AVERAGE_RATE * averages[param_index] + (1.0 - AVERAGE_RATE) * master_new
        updates.append((gradient, master_new, moment_new, average_new, master_new.astype(jnp.bfloat16)))
    return (joint_rows, input_grad, updates[0][0], updates[0][1], updates[0][2], updates[0][3], updates[0][4], updates[1][0], updates[1][1], updates[1][2], updates[1][3], updates[1][4], updates[2][0], updates[2][1], updates[2][2], updates[2][3], updates[2][4], updates[3][0], updates[3][1], updates[3][2], updates[3][3], updates[3][4], updates[4][0], updates[4][1], updates[4][2], updates[4][3], updates[4][4])
```

```python
import functools
import math

import jax
import jax.numpy as jnp
from jax import lax
from jax.experimental import pallas as pl
from jax.experimental.pallas import tpu as pltpu
from jax.sharding import PartitionSpec as P

HD = 64
PAIR = 2 * HD
EPSILON = 1e-06
MOMENTUM = 0.9
AVERAGE_RATE = 0.6
STEP_RATES = (0.013, 1.3, 0.06, 0.015, 0.04)
SPLIT = 8
BF = jnp.bfloat16
F32 = jnp.float32
VMEM_BYTES = 56 * 1024 * 1024


def dot(left, right):
    return lax.dot_general(left, right, (((1,), (0,)), ((), ())), preferred_element_type=F32)


def dot_t(left, right):
    return lax.dot_general(left, right, (((1,), (1,)), ((), ())), preferred_element_type=F32)


def t_dot(left, right):
    return lax.dot_general(left, right, (((0,), (0,)), ((), ())), preferred_element_type=F32)


def unit_and_scale(rows):
    centred = rows - jnp.mean(rows, axis=-1, keepdims=True)
    spread = jnp.mean(centred * centred, axis=-1, keepdims=True)
    scale = lax.rsqrt(spread + EPSILON)
    return centred * scale, scale


def norm_back(grad_out, unit, scale, gain):
    grad_unit = grad_out * gain
    inner = jnp.mean(grad_unit, axis=-1, keepdims=True)
    along = jnp.mean(grad_unit * unit, axis=-1, keepdims=True)
    return scale * (grad_unit - inner - unit * along)


def half_masks():
    lane = lax.broadcasted_iota(jnp.int32, (1, PAIR), 1)
    return [jnp.where(lane < HD, 1.0, 0.0).astype(BF), jnp.where(lane < HD, 0.0, 1.0).astype(BF)]


def place_table(order_ref, count, seq, length):
    slot = lax.broadcasted_iota(jnp.int32, (length, length), 0)
    lane = lax.broadcasted_iota(jnp.int32, (length, length), 1)
    own = jnp.where(lax.axis_index("tower") == 0, order_ref[seq : seq + 1, :], lane[0:1, :])
    return jnp.where((slot == own) & (lane < count), 1.0, 0.0).astype(BF)


def front_kernel(
    seq, order_ref, count_ref, x_ref, win_ref, norm_ref, rows_ref, first_ref, qkv_ref, probs_ref, ctx_ref
):
    length = x_ref.shape[1]
    inner = win_ref.shape[2]
    count = count_ref[0, seq]
    table = place_table(order_ref, count, seq, length)
    rows = t_dot(table, x_ref[0])
    rows_ref[...] = rows.astype(BF)
    unit, _ = unit_and_scale(rows)
    norms = norm_ref[...].astype(F32)
    first = (unit * norms[0:1] + norms[1:2]).astype(BF)
    first_ref[...] = first
    for part in range(3):
        qkv_ref[part] = dot(first, win_ref[part]).astype(BF)
    masks = half_masks()
    key_lane = lax.broadcasted_iota(jnp.int32, (1, length), 1) < count
    for pair in range(inner // PAIR):
        cols = pl.ds(pair * PAIR, PAIR)
        queries = qkv_ref[0, :, cols]
        keys = qkv_ref[1, :, cols]
        values = qkv_ref[2, :, cols]
        probs = []
        for half in range(2):
            scores = dot_t(queries * (masks[half] * HD**-0.5).astype(BF), keys)
            scores = jnp.where(key_lane, scores, -1e30)
            top = jnp.max(scores, axis=-1, keepdims=True)
            powers = jnp.exp(scores - top)
            total = jnp.sum(powers, axis=-1, keepdims=True)
            low = (powers * (1.0 / total)).astype(BF)
            probs_ref[2 * pair + half] = low
            probs.append(low)
        stacked = jnp.concatenate([values * masks[0], values * masks[1]], axis=0)
        ctx_ref[:, cols] = dot(jnp.concatenate(probs, axis=1), stacked).astype(BF)


def mid_kernel(
    seq,
    count_ref,
    rows_ref,
    ctx_ref,
    ctx_other_ref,
    wout_ref,
    wout_other_ref,
    norm_ref,
    wup_ref,
    wdown_ref,
    cot_ref,
    cot_other_ref,
    middle_ref,
    second_ref,
    final_ref,
    hidden_ref,
    pre_ref,
    back_ref,
    out_ref,
):
    length = rows_ref.shape[0]
    hidden_width = wup_ref.shape[1]
    low_side = lax.axis_index("mp") == 0
    ctx, other = ctx_ref[...], ctx_other_ref[...]
    wout, wother = wout_ref[...], wout_other_ref[...]
    both = jnp.concatenate(
        [jnp.where(low_side, ctx, other), jnp.where(low_side, other, ctx)], axis=1
    )
    weights = jnp.concatenate(
        [jnp.where(low_side, wout, wother), jnp.where(low_side, wother, wout)], axis=0
    )
    middle = rows_ref[...].astype(F32) + dot(both, weights)
    middle_ref[...] = middle
    unit, _ = unit_and_scale(middle)
    norms = norm_ref[...].astype(F32)
    second = (unit * norms[2:3] + norms[3:4]).astype(BF)
    second_ref[...] = second
    valid = lax.broadcasted_iota(jnp.int32, (length, 1), 0) < count_ref[0, seq]
    cot = jnp.where(lax.axis_index("tower") == seq, cot_ref[0], cot_other_ref[...])
    grad_final = jnp.where(valid, cot.astype(F32), 0.0).astype(BF)
    final_ref[...] = grad_final
    tile = 256
    for step in range(hidden_width // tile):
        cols = pl.ds(step * tile, tile)
        pre = dot(second, wup_ref[:, cols])
        grad_hidden = dot_t(grad_final, wdown_ref[cols, :])
        power = jnp.exp(pre * pre * -0.5)
        reach = 1.0 / (1.0 + jnp.abs(pre) * (0.3275911 / math.sqrt(2.0)))
        tail = (
            reach
            * (
                0.127414796
                + reach
                * (
                    -0.142248368
                    + reach * (0.7107068705 + reach * (-0.7265760135 + reach * 0.5307027145))
                )
            )
            * power
        )
        phi = jnp.where(pre >= 0.0, 1.0 - tail, tail)
        hidden_ref[:, cols] = (pre * phi).astype(BF)
        slope = phi + pre * (power * (1.0 / math.sqrt(2.0 * math.pi)))
        pre_ref[:, cols] = (grad_hidden * slope).astype(BF)
    back_ref[...] = dot_t(pre_ref[...], wup_ref[...]).astype(BF)
    out_ref[...] = dot(hidden_ref[...], wdown_ref[...]).astype(BF)


def block_home(own, block, order):
    which = 1 - ((block >> order[0]) & 1) if own else (block >> order[0]) & 1
    return which, 2 * ((block >> order[1]) & 1) + ((block >> order[2]) & 1)


def store_blocks(order, stride, left, left_scr):
    rows = left.shape[0] // SPLIT
    own = (lax.axis_index("dp") // (stride << order[0])) & 1
    for side in range(2):

        @pl.when(own == side)
        def _():
            for block in range(SPLIT):
                which, place = block_home(side, block, order)
                left_scr[which, place * rows : (place + 1) * rows, :] = left[
                    block * rows : (block + 1) * rows
                ]


def grads_kernel(order, stride, lefts, rights, keep_ref, send_ref, left_scr):
    @pl.when(pl.program_id(0) == 0)
    def _():
        left = jnp.concatenate([ref[...].T for ref in lefts], axis=1)
        store_blocks(order, stride, left, left_scr)

    right = jnp.concatenate([ref[...] for ref in rights], axis=0)
    send_ref[...] = dot(left_scr[1], right).astype(BF)
    keep_ref[...] = dot(left_scr[0], right).astype(BF)


def mixer_grads_kernel(
    order, stride, mid_refs, ctx_refs, first_refs, mixed_refs, keep_ref, send_ref, mid_scr, first_scr
):
    inner = ctx_refs[0].shape[1]
    store_blocks(order, stride, jnp.concatenate([r[...].T for r in mid_refs], axis=1), mid_scr)
    store_blocks(order, stride, jnp.concatenate([r[...].T for r in first_refs], axis=1), first_scr)
    right = jnp.concatenate([r[...] for r in ctx_refs], axis=0)
    mixed = [jnp.concatenate([r[part] for r in mixed_refs], axis=0) for part in range(3)]
    for which, ref in ((1, send_ref), (0, keep_ref)):
        ref[:, 3 * inner : 4 * inner] = dot(mid_scr[which], right).astype(BF)
        for part in range(3):
            ref[:, part * inner : (part + 1) * inner] = dot(first_scr[which], mixed[part]).astype(BF)


def back_kernel(
    own_ref,
    other_ref,
    middle_ref,
    final_ref,
    norm_ref,
    wout_ref,
    win_ref,
    qkv_ref,
    probs_ref,
    mid_ref,
    mixed_ref,
    first_ref,
    norm_grad_ref,
    ctx_grad_scr,
):
    inner = wout_ref.shape[0]
    grad_second = own_ref[...].astype(F32) + other_ref[...].astype(F32)
    unit, scale = unit_and_scale(middle_ref[...])
    norm_grad_ref[0:1] = jnp.sum(grad_second * unit, axis=0, keepdims=True)
    norm_grad_ref[1:2] = jnp.sum(grad_second, axis=0, keepdims=True)
    gain = norm_ref[2:3].astype(F32)
    grad_mid = final_ref[...].astype(F32) + norm_back(grad_second, unit, scale, gain)
    grad_mid = grad_mid.astype(BF)
    mid_ref[...] = grad_mid
    ctx_grad_scr[...] = dot_t(grad_mid, wout_ref[...]).astype(BF)
    masks = half_masks()
    for pair in range(inner // PAIR):
        cols = pl.ds(pair * PAIR, PAIR)
        queries = qkv_ref[0, :, cols]
        keys = qkv_ref[1, :, cols]
        values = qkv_ref[2, :, cols]
        grad_ctx = ctx_grad_scr[:, cols]
        halves = [grad_ctx * masks[0], grad_ctx * masks[1]]
        probs, slopes = [], []
        for half in range(2):
            low = probs_ref[2 * pair + half]
            prob = low.astype(F32)
            grad_probs = dot_t(halves[half], values)
            along = jnp.sum(prob * grad_probs, axis=-1, keepdims=True)
            slopes.append((prob * (grad_probs - along)).astype(BF))
            probs.append(low)
        key_stack = jnp.concatenate([keys * masks[0], keys * masks[1]], axis=0)
        query_stack = jnp.concatenate([queries * masks[0], queries * masks[1]], axis=0)
        grad_q = dot(jnp.concatenate(slopes, axis=1), key_stack) * HD**-0.5
        grad_k = t_dot(jnp.concatenate(slopes, axis=0), query_stack) * HD**-0.5
        grad_v = t_dot(jnp.concatenate(probs, axis=0), jnp.concatenate(halves, axis=0))
        mixed_ref[0, :, cols] = grad_q.astype(BF)
        mixed_ref[1, :, cols] = grad_k.astype(BF)
        mixed_ref[2, :, cols] = grad_v.astype(BF)
    total = dot_t(mixed_ref[0], win_ref[0])
    for part in range(1, 3):
        total += dot_t(mixed_ref[part], win_ref[part])
    first_ref[...] = total.astype(BF)


def input_kernel(
    order_ref, count_ref, own_refs, other_refs, rows_refs, mid_refs, norm_ref, seconds, out_ref, norm_grad_ref
):
    length = rows_refs[0].shape[0]
    gain = norm_ref[0:1].astype(F32)
    gains, shifts = [], []
    for seq in range(len(rows_refs)):
        grad_first = own_refs[seq][...].astype(F32) + other_refs[seq][...].astype(F32)
        unit, scale = unit_and_scale(rows_refs[seq][...].astype(F32))
        gains.append(jnp.sum(grad_first * unit, axis=0, keepdims=True))
        shifts.append(jnp.sum(grad_first, axis=0, keepdims=True))
        grad_rows = mid_refs[seq][...].astype(F32) + norm_back(grad_first, unit, scale, gain)
        table = place_table(order_ref, count_ref[0, seq], seq, length)
        out_ref[0, seq] = dot(table, grad_rows.astype(BF)).astype(BF)
    norm_grad_ref[0:1] = functools.reduce(jnp.add, gains)
    norm_grad_ref[1:2] = functools.reduce(jnp.add, shifts)
    norm_grad_ref[2:4] = functools.reduce(jnp.add, [r[...] for r in seconds])


def final_kernel(count_ref, middle_refs, own_refs, other_refs, keep_ref, send_ref):
    length = middle_refs[0].shape[0]
    row = lax.broadcasted_iota(jnp.int32, (length, 1), 0)
    tower = lax.axis_index("tower")
    for seq in range(2):
        output = own_refs[seq][...].astype(F32) + other_refs[seq][...].astype(F32)
        final = jnp.where(row < count_ref[0, seq], middle_refs[seq][...] + output, 0.0).astype(BF)

        @pl.when(tower == seq)
        def _():
            keep_ref[...] = final

        @pl.when(tower != seq)
        def _():
            send_ref[...] = final


def update_values(gradient, master, moment, average, rate):
    moment_new = MOMENTUM * moment + gradient
    master_new = master - rate * (gradient + MOMENTUM * moment_new)
    average_new = AVERAGE_RATE * average + (1.0 - AVERAGE_RATE) * master_new
    return gradient, master_new, moment_new, average_new, master_new.astype(BF)


def update_kernel(rate, grad_ref, master_ref, moment_ref, average_ref, *outs):
    values = update_values(
        grad_ref[...], master_ref[...], moment_ref[...], average_ref[...], rate
    )
    for ref, value in zip(outs, values):
        ref[...] = value


def call(kernel, outs, *args, smem=(), scratch=(), flops=0, transcendentals=0):
    flat, tree = jax.tree.flatten(args)
    out_flat = [jax.ShapeDtypeStruct(s, d) for s, d in outs]
    scalar = [any(a is b for b in smem) for a in flat]
    moved = sum(a.size * a.dtype.itemsize for a in list(flat) + out_flat)

    def body(*refs):
        ins = jax.tree.unflatten(tree, refs[: len(flat)])
        kernel(*ins, *refs[len(flat) :])

    return pl.pallas_call(
        body,
        out_shape=out_flat,
        in_specs=[
            pl.BlockSpec(memory_space=pltpu.SMEM if s else pltpu.VMEM) for s in scalar
        ],
        out_specs=[pl.BlockSpec(memory_space=pltpu.VMEM) for _ in outs],
        scratch_shapes=list(scratch),
        compiler_params=pltpu.CompilerParams(vmem_limit_bytes=VMEM_BYTES),
        cost_estimate=pl.CostEstimate(
            flops=flops, transcendentals=transcendentals, bytes_accessed=moved
        ),
    )(*flat)


def swap(values, axis):
    return lax.ppermute(values, axis, [(0, 1), (1, 0)])


def hop(values, bit, stride):
    size = lax.axis_size("dp")
    step = stride << bit
    return lax.ppermute(values, "dp", [(i, i ^ step) for i in range(size)])


def take(values, index):
    return lax.dynamic_index_in_dim(values, index, 0, keepdims=False).astype(F32)


def reduce_chunk(keep, send, order, stride):
    rows = keep.shape[0] // 4
    width = keep.shape[1]
    index = lax.axis_index("dp") // stride
    bit_two = (index >> order[1]) & 1
    bit_three = (index >> order[2]) & 1
    keep = keep.reshape(2, 2, rows, width)
    one = hop(send, order[0], stride).reshape(2, 2, rows, width)
    send_two = (take(keep, 1 - bit_two) + take(one, 1 - bit_two)).astype(BF)
    two = hop(send_two, order[1], stride)
    keep_own, one_own = take(keep, bit_two), take(one, bit_two)
    send_three = (
        take(keep_own, 1 - bit_three) + take(one_own, 1 - bit_three) + take(two, 1 - bit_three)
    ).astype(BF)
    three = hop(send_three, order[2], stride)
    total = take(keep_own, bit_three) + take(one_own, bit_three) + take(two, bit_three)
    total = total + three.astype(F32)
    if stride > 1:
        size = lax.axis_size("dp")
        groups = [[g * stride + i for i in range(stride)] for g in range(size // stride)]
        total = lax.psum_scatter(
            total, "dp", scatter_dimension=0, axis_index_groups=groups, tiled=True
        )
    return total


def gradient_halves(lefts, rights, order, stride):
    tokens = sum(r.shape[0] for r in lefts)
    width = lefts[0].shape[1]
    columns = rights[0].shape[1]
    tile = 512
    count = len(lefts)

    def body(*refs):
        grads_kernel(order, stride, refs[:count], refs[count : 2 * count], *refs[2 * count :])

    half = jax.ShapeDtypeStruct((width // 2, columns), BF)
    return pl.pallas_call(
        body,
        out_shape=[half, half],
        grid=(columns // tile,),
        in_specs=[pl.BlockSpec(r.shape, lambda i: (0, 0)) for r in lefts]
        + [pl.BlockSpec((r.shape[0], tile), lambda i: (0, i)) for r in rights],
        out_specs=[pl.BlockSpec((width // 2, tile), lambda i: (0, i))] * 2,
        scratch_shapes=[pltpu.VMEM((2, width // 2, tokens), BF)],
        compiler_params=pltpu.CompilerParams(
            vmem_limit_bytes=VMEM_BYTES, dimension_semantics=("arbitrary",)
        ),
        cost_estimate=pl.CostEstimate(
            flops=2 * tokens * width * columns,
            transcendentals=0,
            bytes_accessed=2 * (width * columns + tokens * (width + columns)),
        ),
    )(*lefts, *rights)


def shards(
    tower_input,
    patch_order,
    visible_count,
    joint_cotangent,
    mixer_in_copy,
    mixer_in_master,
    mixer_in_moment,
    mixer_in_average,
    mixer_out_copy,
    mixer_out_master,
    mixer_out_moment,
    mixer_out_average,
    expand_copy,
    expand_master,
    expand_moment,
    expand_average,
    contract_copy,
    contract_master,
    contract_moment,
    contract_average,
    norm_params_copy,
    norm_params_master,
    norm_params_moment,
    norm_params_average,
):
    seq_count, length, width = tower_input.shape[1:]
    inner = mixer_in_copy.shape[3]
    heads = inner // HD
    hidden_width = expand_copy.shape[2]
    dp_size = lax.axis_size("dp")
    stride = dp_size // SPLIT
    tower = lax.axis_index("tower")
    w_in = jnp.transpose(mixer_in_copy[0], (1, 0, 2))
    w_out, w_up, w_down = mixer_out_copy[0], expand_copy[0], contract_copy[0]
    norms = norm_params_copy[0]
    x = tower_input[0]
    cot = joint_cotangent.reshape(2, length, width)
    w_out_other = swap(w_out, "mp")
    cot_other = swap(lax.dynamic_index_in_dim(cot, 1 - tower, 0, keepdims=False), "tower")

    act = (length, width)
    fronts = []
    for seq in range(2):
        fronts.append(
            call(
                functools.partial(front_kernel, seq),
                [
                    (act, BF),
                    (act, BF),
                    ((3, length, inner), BF),
                    ((heads, length, length), BF),
                    ((length, inner), BF),
                ],
                patch_order,
                visible_count,
                x[seq : seq + 1],
                w_in,
                norms,
                smem=(visible_count,),
                flops=2 * length * width * (3 * inner + length) + 8 * heads * length * length * HD,
                transcendentals=heads * length * length,
            )
        )
    rows, firsts, qkvs, probs, ctxs = zip(*fronts)
    mids = []
    for seq in range(2):
        ctx_other = swap(ctxs[seq], "mp")
        mids.append(
            call(
                functools.partial(mid_kernel, seq),
                [
                    (act, F32),
                    (act, BF),
                    (act, BF),
                    ((length, hidden_width), BF),
                    ((length, hidden_width), BF),
                    (act, BF),
                    (act, BF),
                ],
                visible_count,
                rows[seq],
                ctxs[seq],
                ctx_other,
                w_out,
                w_out_other,
                norms,
                w_up,
                w_down,
                cot[seq : seq + 1],
                cot_other,
                smem=(visible_count,),
                flops=2 * length * width * (4 * hidden_width + 2 * inner),
                transcendentals=2 * length * hidden_width,
            )
        )
    middles, seconds, finals, hiddens, pres, backs, outs = zip(*mids)
    backs_other = [swap(b, "mp") for b in backs]

    order_a, order_b = (0, 1, 2), (1, 0, 2)
    down_keep, down_send = gradient_halves(finals, hiddens, order_a, stride)
    down_sum = reduce_chunk(down_keep, down_send, order_a, stride)
    up_keep, up_send = gradient_halves(seconds, pres, order_b, stride)
    up_sum = reduce_chunk(up_keep, up_send, order_b, stride)

    lasts = []
    for seq in range(2):
        lasts.append(
            call(
                back_kernel,
                [(act, BF), ((3, length, inner), BF), (act, BF), ((2, width), F32)],
                backs[seq],
                backs_other[seq],
                middles[seq],
                finals[seq],
                norms,
                w_out,
                w_in,
                qkvs[seq],
                probs[seq],
                scratch=[pltpu.VMEM((length, inner), BF)],
                flops=2 * length * width * 4 * inner + 16 * heads * length * length * HD,
            )
        )
    grad_mids, mixeds, grad_firsts, second_norm_grads = zip(*lasts)
    grad_firsts_other = [swap(g, "mp") for g in grad_firsts]
    tokens = seq_count * length
    half = ((width // 2, 4 * inner), BF)
    mixer_keep, mixer_send = call(
        functools.partial(mixer_grads_kernel, order_a, stride),
        [half, half],
        list(grad_mids),
        list(ctxs),
        list(firsts),
        list(mixeds),
        scratch=[pltpu.VMEM((2, width // 2, tokens), BF)] * 2,
        flops=2 * tokens * width * 4 * inner,
    )
    mixer_sum = reduce_chunk(mixer_keep, mixer_send, order_a, stride)

    outs_other = [swap(o, "mp") for o in outs]
    row_keep, row_send = call(
        final_kernel,
        [(act, BF), (act, BF)],
        visible_count,
        list(middles),
        list(outs),
        outs_other,
        smem=(visible_count,),
    )
    row_other = swap(row_send, "tower")
    joint_rows = jnp.where(
        tower == 0, jnp.stack([row_keep, row_other]), jnp.stack([row_other, row_keep])
    ).reshape(1, 1, 2, seq_count // 2, length, width)

    input_grad, norm_grads = call(
        input_kernel,
        [((1, seq_count, length, width), BF), ((4, width), F32)],
        patch_order,
        visible_count,
        list(grad_firsts),
        grad_firsts_other,
        list(rows),
        list(grad_mids),
        norms,
        list(second_norm_grads),
        smem=(visible_count,),
    )
    norm_parts = lax.all_to_all(
        jnp.transpose(norm_grads.reshape(4, dp_size, width // dp_size), (1, 0, 2)),
        "dp",
        split_axis=0,
        concat_axis=0,
        tiled=True,
    )
    norm_sum = jnp.sum(norm_parts, axis=0)

    rate_scale = 1.0 / math.sqrt(seq_count * dp_size * length)

    def update(total, master, moment, average, index):
        return call(
            functools.partial(update_kernel, STEP_RATES[index] * rate_scale),
            [(total.shape, F32)] * 4 + [(total.shape, BF)],
            total,
            master,
            moment,
            average,
        )

    def turned(values):
        return jnp.transpose(values[0], (1, 0, 2))

    shard = mixer_sum.shape[0]
    in_total = jnp.transpose(mixer_sum[:, : 3 * inner].reshape(shard, 3, inner), (1, 0, 2))
    in_set = update(
        in_total, turned(mixer_in_master), turned(mixer_in_moment), turned(mixer_in_average), 0
    )
    out_set = update(
        mixer_sum[:, 3 * inner :],
        mixer_out_master[0].T,
        mixer_out_moment[0].T,
        mixer_out_average[0].T,
        1,
    )
    up_set = update(up_sum, expand_master[0], expand_moment[0], expand_average[0], 2)
    down_set = update(
        down_sum, contract_master[0].T, contract_moment[0].T, contract_average[0].T, 3
    )
    norm_set = update_values(
        norm_sum[None],
        norm_params_master,
        norm_params_moment,
        norm_params_average,
        STEP_RATES[4] * rate_scale,
    )
    return (
        joint_rows,
        input_grad,
        *[jnp.transpose(v, (1, 0, 2))[None] for v in in_set],
        *[v.T[None] for v in out_set],
        *[v[None] for v in up_set],
        *[v.T[None] for v in down_set],
        *norm_set,
    )


def solution(mesh):
    weight_in = P("tower", "dp", None, "mp")
    weight_out = P("tower", "mp", "dp")
    weight_up = P("tower", "dp", "mp")
    norm = P("tower", None, "dp")
    return jax.shard_map(
        shards,
        mesh=mesh,
        in_specs=(
            P("tower", "dp", None, None),
            P("dp", None),
            P("tower", "dp"),
            P("dp", "tower", None, None, None, None),
            P("tower", None, None, "mp"),
            *[weight_in] * 3,
            P("tower", "mp", None),
            *[weight_out] * 3,
            P("tower", None, "mp"),
            *[weight_up] * 3,
            P("tower", "mp", None),
            *[weight_out] * 3,
            P("tower", None, None),
            *[norm] * 3,
        ),
        out_specs=(
            P("dp", "tower", None, None, None, None),
            P("tower", "dp", None, None),
            *[weight_in] * 5,
            *[weight_out] * 5,
            *[weight_up] * 5,
            *[weight_out] * 5,
            *[norm] * 5,
        ),
        check_vma=False,
    )
```

```python
import functools
import math

import jax
import jax.numpy as jnp
from jax import lax
from jax.experimental import pallas as pl
from jax.experimental.pallas import tpu as pltpu
from jax.sharding import PartitionSpec as P

HD = 64
PAIR = 2 * HD
EPSILON = 1e-06
MOMENTUM = 0.9
AVERAGE_RATE = 0.6
STEP_RATES = (0.013, 1.3, 0.06, 0.015, 0.04)
SPLIT = 8
STEP_WEIGHT = 0
BF = jnp.bfloat16
F32 = jnp.float32
VMEM_BYTES = 6 * 1024 * 1024


def dot(left, right):
    return lax.dot_general(left, right, (((1,), (0,)), ((), ())), preferred_element_type=F32)


def dot_t(left, right):
    return lax.dot_general(left, right, (((1,), (1,)), ((), ())), preferred_element_type=F32)


def t_dot(left, right):
    return lax.dot_general(left, right, (((0,), (0,)), ((), ())), preferred_element_type=F32)


def unit_and_scale(rows):
    centred = rows - jnp.mean(rows, axis=-1, keepdims=True)
    spread = jnp.mean(centred * centred, axis=-1, keepdims=True)
    scale = lax.rsqrt(spread + EPSILON)
    return centred * scale, scale


def norm_back(grad_out, unit, scale, gain):
    grad_unit = grad_out * gain
    inner = jnp.mean(grad_unit, axis=-1, keepdims=True)
    along = jnp.mean(grad_unit * unit, axis=-1, keepdims=True)
    return scale * (grad_unit - inner - unit * along)


def half_masks():
    lane = lax.broadcasted_iota(jnp.int32, (1, PAIR), 1)
    return [jnp.where(lane < HD, 1.0, 0.0).astype(BF), jnp.where(lane < HD, 0.0, 1.0).astype(BF)]


def place_table(order_ref, count, seq, length):
    slot = lax.broadcasted_iota(jnp.int32, (length, length), 0)
    lane = lax.broadcasted_iota(jnp.int32, (length, length), 1)
    own = jnp.where(lax.axis_index("tower") == 0, order_ref[seq : seq + 1, :], lane[0:1, :])
    return jnp.where((slot == own) & (lane < count), 1.0, 0.0).astype(BF)


def front_kernel(
    seq,
    order_ref,
    count_ref,
    x_ref,
    win_ref,
    norm_ref,
    rows_ref,
    first_ref,
    qkv_ref,
    probs_ref,
    ctx_ref,
):
    length = x_ref.shape[1]
    inner = win_ref.shape[2]
    count = count_ref[0:1, seq : seq + 1]
    table = place_table(order_ref, count, seq, length)
    rows = t_dot(table, x_ref[seq])
    rows_ref[...] = rows.astype(BF)
    unit, _ = unit_and_scale(rows)
    norms = norm_ref[...].astype(F32)
    first = (unit * norms[0:1] + norms[1:2]).astype(BF)
    first_ref[...] = first
    for part in range(3):
        qkv_ref[part] = dot(first, win_ref[part]).astype(BF)
    masks = half_masks()
    key_lane = lax.broadcasted_iota(jnp.int32, (1, length), 1) < count
    for pair in range(inner // PAIR):
        cols = pl.ds(pair * PAIR, PAIR)
        queries = qkv_ref[0, :, cols]
        keys = qkv_ref[1, :, cols]
        values = qkv_ref[2, :, cols]
        probs = []
        for half in range(2):
            scores = dot_t(queries * (masks[half] * HD**-0.5).astype(BF), keys)
            scores = jnp.where(key_lane, scores, -1e30)
            top = jnp.max(scores, axis=-1, keepdims=True)
            powers = jnp.exp(scores - top)
            total = jnp.sum(powers, axis=-1, keepdims=True)
            low = (powers * (1.0 / total)).astype(BF)
            probs_ref[2 * pair + half] = low
            probs.append(low)
        stacked = jnp.concatenate([values * masks[0], values * masks[1]], axis=0)
        ctx_ref[:, cols] = dot(jnp.concatenate(probs, axis=1), stacked).astype(BF)


def fetch(far_refs, near_refs, sems):
    copies = [
        pltpu.make_async_copy(far, close, sems.at[i])
        for i, (far, close) in enumerate(zip(far_refs, near_refs))
    ]
    for copy in copies:
        copy.start()
    return copies


def attend(ctx_ref, wout_ref, att_ref):
    att_ref[...] = dot(ctx_ref[...], wout_ref[...]).astype(BF)


def lead_kernel(*refs):
    far_refs, near_refs, refs = refs[:7], refs[7:14], refs[14:]
    order_ref, count_ref, x_ref, win_ref, norm_ref, wout_ref, cot_ref = near_refs
    att_ref, cot_send_ref, *rest, sems = refs
    copies = fetch(far_refs, near_refs, sems)
    for place in range(5):
        copies[place].wait()
    front_kernel(0, order_ref, count_ref, x_ref, win_ref, norm_ref, *rest)
    copies[5].wait()
    attend(rest[-1], wout_ref, att_ref)
    copies[6].wait()
    cot_send_ref[...] = cot_ref[1 - lax.axis_index("tower")]


def next_kernel(*refs):
    far_refs, ins, near_refs, refs = refs[:2], refs[2:8], refs[8:10], refs[10:]
    att_ref, *rest, sems = refs
    copies = fetch(far_refs, near_refs, sems)
    front_kernel(1, *ins[:5], *rest)
    attend(rest[-1], ins[5], att_ref)
    for copy in copies:
        copy.wait()


def fetch_kernel(*refs):
    count = len(refs) // 2
    for copy in fetch(refs[:count], refs[count : 2 * count], refs[-1]):
        copy.wait()


def mid_kernel(
    seq,
    count_ref,
    rows_ref,
    att_ref,
    att_other_ref,
    norm_ref,
    wup_ref,
    wdown_ref,
    cot_ref,
    cot_other_ref,
    back_ref,
    out_ref,
    middle_ref,
    second_ref,
    final_ref,
    hidden_ref,
    pre_ref,
):
    length = rows_ref.shape[0]
    hidden_width = wup_ref.shape[1]
    attended = att_ref[...].astype(F32) + att_other_ref[...].astype(F32)
    middle = rows_ref[...].astype(F32) + attended
    middle_ref[...] = middle
    unit, _ = unit_and_scale(middle)
    norms = norm_ref[...].astype(F32)
    second = (unit * norms[2:3] + norms[3:4]).astype(BF)
    second_ref[...] = second
    valid = lax.broadcasted_iota(jnp.int32, (length, 1), 0) < count_ref[0:1, seq : seq + 1]
    cot = jnp.where(lax.axis_index("tower") == seq, cot_ref[seq], cot_other_ref[...])
    grad_final = jnp.where(valid, cot.astype(F32), 0.0).astype(BF)
    final_ref[...] = grad_final
    tile = 256
    for step in range(hidden_width // tile):
        cols = pl.ds(step * tile, tile)
        pre = dot(second, wup_ref[:, cols])
        grad_hidden = dot_t(grad_final, wdown_ref[cols, :])
        power = jnp.exp(pre * pre * -0.5)
        reach = 1.0 / (1.0 + jnp.abs(pre) * (0.3275911 / math.sqrt(2.0)))
        tail = (
            reach
            * (
                0.127414796
                + reach
                * (
                    -0.142248368
                    + reach * (0.7107068705 + reach * (-0.7265760135 + reach * 0.5307027145))
                )
            )
            * power
        )
        phi = jnp.where(pre >= 0.0, 1.0 - tail, tail)
        hidden_ref[:, cols] = (pre * phi).astype(BF)
        slope = phi + pre * (power * (1.0 / math.sqrt(2.0 * math.pi)))
        pre_ref[:, cols] = (grad_hidden * slope).astype(BF)
    back_ref[...] = dot_t(pre_ref[...], wup_ref[...]).astype(BF)
    out_ref[...] = dot(hidden_ref[...], wdown_ref[...]).astype(BF)


def block_home(own, block, order):
    which = 1 - ((block >> order[0]) & 1) if own else (block >> order[0]) & 1
    return which, 2 * ((block >> order[1]) & 1) + ((block >> order[2]) & 1)


def store_blocks(order, stride, left, left_scr):
    rows = left.shape[0] // SPLIT
    own = (lax.axis_index("dp") // (stride << order[0])) & 1
    for side in range(2):

        @pl.when(own == side)
        def _():
            for block in range(SPLIT):
                which, place = block_home(side, block, order)
                left_scr[which, place * rows : (place + 1) * rows, :] = left[
                    block * rows : (block + 1) * rows
                ]


def grads_kernel(order, stride, lefts, rights, keep_ref, send_ref, left_scr):
    store_blocks(order, stride, jnp.concatenate([r[...].T for r in lefts], axis=1), left_scr)
    right = jnp.concatenate([r[...] for r in rights], axis=0)
    send_ref[...] = dot(left_scr[1], right).astype(BF).reshape(send_ref.shape)
    keep_ref[...] = dot(left_scr[0], right).astype(BF).reshape(keep_ref.shape)


def mixer_a_kernel(
    order,
    stride,
    first_refs,
    mixed_refs,
    norm_own_ref,
    norm_other_ref,
    out_refs,
    grad_first_refs,
    keep_ref,
    send_ref,
    outs_ref,
    grads_ref,
    first_scr,
):
    for seq in range(2):
        outs_ref[seq] = out_refs[seq][...]
        grads_ref[seq] = grad_first_refs[seq][...]
    inner = mixed_refs[0].shape[2]
    store_blocks(order, stride, jnp.concatenate([r[...].T for r in first_refs], axis=1), first_scr)
    rows = first_scr.shape[1] // 4
    shape = (2, 2, rows, inner)
    mixed = [jnp.concatenate([r[part] for r in mixed_refs], axis=0) for part in range(2)]
    for which, ref in ((1, send_ref), (0, keep_ref)):
        for part in range(2):
            cols = slice(part * inner, (part + 1) * inner)
            ref[:, :, 0:rows, cols] = dot(first_scr[which], mixed[part]).astype(BF).reshape(shape)
        ref[:, :, rows:, :] = jnp.zeros((2, 2, 8, 2 * inner), BF)
    own_norm = norm_own_ref[...]
    row = lax.broadcasted_iota(jnp.int32, (8, 1), 0)
    norm_grad = own_norm + jnp.where(row < 2, norm_other_ref[...], 0.0)
    own = own_bit(order, 0, stride)
    for block in range(SPLIT):
        piece = norm_grad[:, block * rows : (block + 1) * rows].astype(BF)
        bits = [(block >> o) & 1 for o in order]

        @pl.when(own == bits[0])
        def _():
            keep_ref[bits[1], bits[2], rows:, 0:rows] = piece

        @pl.when(own != bits[0])
        def _():
            send_ref[bits[1], bits[2], rows:, 0:rows] = piece


def mixer_b_kernel(
    order,
    stride,
    mid_refs,
    ctx_refs,
    first_refs,
    mixed_refs,
    keep_ref,
    send_ref,
    first_scr,
    mid_scr,
):
    inner = ctx_refs[0].shape[1]
    store_blocks(order, stride, jnp.concatenate([r[...].T for r in first_refs], axis=1), first_scr)
    store_blocks(order, stride, jnp.concatenate([r[...].T for r in mid_refs], axis=1), mid_scr)
    right = jnp.concatenate([r[...] for r in ctx_refs], axis=0)
    mixed = jnp.concatenate([r[2] for r in mixed_refs], axis=0)
    shape = keep_ref.shape[:3] + (inner,)
    for which, ref in ((1, send_ref), (0, keep_ref)):
        ref[:, :, :, 0:inner] = dot(first_scr[which], mixed).astype(BF).reshape(shape)
        ref[:, :, :, inner : 2 * inner] = dot(mid_scr[which], right).astype(BF).reshape(shape)


def back_kernel(
    own_ref,
    other_ref,
    middle_ref,
    final_ref,
    norm_ref,
    wout_ref,
    win_ref,
    qkv_ref,
    probs_ref,
    rows_ref,
    before_ref,
    first_ref,
    mid_ref,
    mixed_ref,
    norm_grad_ref,
    ctx_grad_scr,
):
    inner = wout_ref.shape[0]
    grad_second = own_ref[...].astype(F32) + other_ref[...].astype(F32)
    unit, scale = unit_and_scale(middle_ref[...])
    second_gain = jnp.sum(grad_second * unit, axis=0, keepdims=True)
    second_shift = jnp.sum(grad_second, axis=0, keepdims=True)
    gain = norm_ref[2:3].astype(F32)
    grad_mid = final_ref[...].astype(F32) + norm_back(grad_second, unit, scale, gain)
    grad_mid = grad_mid.astype(BF)
    mid_ref[...] = grad_mid
    ctx_grad_scr[...] = dot_t(grad_mid, wout_ref[...]).astype(BF)
    masks = half_masks()
    for pair in range(inner // PAIR):
        cols = pl.ds(pair * PAIR, PAIR)
        queries = qkv_ref[0, :, cols]
        keys = qkv_ref[1, :, cols]
        values = qkv_ref[2, :, cols]
        grad_ctx = ctx_grad_scr[:, cols]
        halves = [grad_ctx * masks[0], grad_ctx * masks[1]]
        probs, slopes = [], []
        for half in range(2):
            low = probs_ref[2 * pair + half]
            prob = low.astype(F32)
            grad_probs = dot_t(halves[half], values)
            along = jnp.sum(prob * grad_probs, axis=-1, keepdims=True)
            slopes.append((prob * (grad_probs - along)).astype(BF))
            probs.append(low)
        key_stack = jnp.concatenate([keys * masks[0], keys * masks[1]], axis=0)
        query_stack = jnp.concatenate([queries * masks[0], queries * masks[1]], axis=0)
        grad_q = dot(jnp.concatenate(slopes, axis=1), key_stack) * HD**-0.5
        grad_k = t_dot(jnp.concatenate(slopes, axis=0), query_stack) * HD**-0.5
        grad_v = t_dot(jnp.concatenate(probs, axis=0), jnp.concatenate(halves, axis=0))
        mixed_ref[0, :, cols] = grad_q.astype(BF)
        mixed_ref[1, :, cols] = grad_k.astype(BF)
        mixed_ref[2, :, cols] = grad_v.astype(BF)
    total = dot_t(mixed_ref[0], win_ref[0])
    for part in range(1, 3):
        total += dot_t(mixed_ref[part], win_ref[part])
    first_ref[...] = total.astype(BF)
    unit, _ = unit_and_scale(rows_ref[...].astype(F32))
    norm_grad = jnp.concatenate(
        [
            jnp.sum(total * unit, axis=0, keepdims=True),
            jnp.sum(total, axis=0, keepdims=True),
            second_gain,
            second_shift,
            jnp.zeros((4, total.shape[1]), F32),
        ],
        axis=0,
    )
    norm_grad_ref[...] = norm_grad if before_ref is None else norm_grad + before_ref[...]


def input_kernel(
    order_ref, count_ref, own_ref, other_ref, rows_refs, mid_refs, norm_ref, out_ref
):
    length = rows_refs[0].shape[0]
    gain = norm_ref[0:1].astype(F32)
    for seq in range(len(rows_refs)):
        grad_first = own_ref[seq].astype(F32) + other_ref[seq].astype(F32)
        unit, scale = unit_and_scale(rows_refs[seq][...].astype(F32))
        grad_rows = mid_refs[seq][...].astype(F32) + norm_back(grad_first, unit, scale, gain)
        table = place_table(order_ref, count_ref[0:1, seq : seq + 1], seq, length)
        out_ref[seq] = dot(table, grad_rows.astype(BF)).astype(BF)


def final_kernel(count_ref, middle_refs, own_ref, other_ref, keep_ref, send_ref):
    length = middle_refs[0].shape[0]
    row = lax.broadcasted_iota(jnp.int32, (length, 1), 0)
    tower = lax.axis_index("tower")
    for seq in range(2):
        output = own_ref[seq].astype(F32) + other_ref[seq].astype(F32)
        final = jnp.where(row < count_ref[0:1, seq : seq + 1], middle_refs[seq][...] + output, 0.0).astype(BF)

        @pl.when(tower == seq)
        def _():
            keep_ref[...] = final

        @pl.when(tower != seq)
        def _():
            send_ref[...] = final


def join_kernel(keep_ref, other_ref, out_ref):
    tower = lax.axis_index("tower")
    out_ref[tower] = keep_ref[...]
    out_ref[1 - tower] = other_ref[...]


def update_values(gradient, master, moment, average, rate):
    moment_new = MOMENTUM * moment + gradient
    master_new = master - rate * (gradient + MOMENTUM * moment_new)
    average_new = AVERAGE_RATE * average + (1.0 - AVERAGE_RATE) * master_new
    return gradient, master_new, moment_new, average_new, master_new.astype(BF)


def update_kernel(rates, orders, stride, chunks, masters, moments, averages, *outs):
    totals, norm_total = [], None
    for order, parts in zip(orders, chunks):
        total = gathered(order, stride, *parts) if len(parts) == 4 else parts[0][...]
        if len(parts) == 2:
            norm_total = parts[1][...]
        rows = masters[0].shape[-2]
        if total.shape[0] > rows:
            norm_total = total[rows : rows + 4, 0:rows]
        totals.append(total[0:rows])
    total = jnp.concatenate(totals, axis=1)
    start = 0
    for place, rate in enumerate(rates):
        group = outs[5 * place : 5 * place + 5]
        deep = masters[place].ndim == 3
        columns = masters[place].shape[-1]
        last = place == 2
        for piece in range(masters[place].shape[0] if deep else 1):
            at = piece if deep else Ellipsis
            values = update_values(
                norm_total if last else total[:, start : start + columns],
                masters[place][at],
                moments[place][at],
                averages[place][at],
                rate,
            )
            for ref, value in zip(group, values):
                ref[at] = value
            start += columns


def near(values):
    return pltpu.with_memory_space_constraint(values, pltpu.VMEM)


class Line:
    def __init__(self):
        self.token = None

    def call(self, kernel, outs, *args, far=0, raw=0, scratch=(), weight=0):
        flat, tree = jax.tree.flatten(args)
        flat = [pltpu.with_memory_space_constraint(v, pltpu.HBM) for v in flat[:raw]] + flat[raw:]
        extra = [] if self.token is None else [self.token]
        near_outs = [pltpu.VMEM(s, d) for s, d in outs[far:]]
        far_outs = [jax.ShapeDtypeStruct(s, d) for s, d in outs[:far]]
        count, gap = len(flat), len(extra)

        def body(*refs):
            ins = jax.tree.unflatten(tree, refs[:count])
            rest = refs[count + gap :]
            kernel(*ins, *rest[: len(outs)], *rest[len(outs) + 1 :])
            rest[len(outs)][...] = jnp.zeros((8, 128), F32)

        whole = pl.BlockSpec(memory_space=pltpu.VMEM)
        *results, self.token = pl.pallas_call(
            body,
            out_shape=far_outs + near_outs + [pltpu.VMEM((8, 128), F32)],
            in_specs=[pl.BlockSpec(memory_space=pltpu.HBM)] * raw + [whole] * (count + gap - raw),
            out_specs=[whole] * (len(outs) + 1),
            scratch_shapes=list(scratch),
            compiler_params=pltpu.CompilerParams(vmem_limit_bytes=VMEM_BYTES),
            cost_estimate=pl.CostEstimate(
                flops=0, transcendentals=0, bytes_accessed=weight
            ),
        )(*flat, *extra)
        return results


def swap(values, axis):
    return near(lax.ppermute(values, axis, [(0, 1), (1, 0)]))


def hop(values, bit, stride):
    size = lax.axis_size("dp")
    step = stride << bit
    return near(lax.ppermute(values, "dp", [(i, i ^ step) for i in range(size)]))


def own_bit(order, stage, stride):
    return (lax.axis_index("dp") // (stride << order[stage])) & 1


def second_kernel(order, stride, keep_ref, one_ref, send_ref):
    other = 1 - own_bit(order, 1, stride)
    total = keep_ref[other].astype(F32) + one_ref[other].astype(F32)
    send_ref[...] = total.astype(send_ref.dtype)


def third_kernel(order, stride, keep_ref, one_ref, two_ref, send_ref):
    own = own_bit(order, 1, stride)
    other = 1 - own_bit(order, 2, stride)
    total = keep_ref[own, other].astype(F32) + one_ref[own, other].astype(F32)
    send_ref[...] = (total + two_ref[other].astype(F32)).astype(send_ref.dtype)


def gathered(order, stride, keep_ref, one_ref, two_ref, three_ref):
    two, three = own_bit(order, 1, stride), own_bit(order, 2, stride)
    total = keep_ref[two, three].astype(F32) + one_ref[two, three].astype(F32)
    return total + two_ref[three].astype(F32) + three_ref[...].astype(F32)


class Chunk:
    def __init__(self, line, keep, send, order, stride):
        self.line, self.order, self.stride = line, order, stride
        self.parts = [keep, hop(send, order[0], stride)]

    def step(self):
        keep = self.parts[0]
        stage = len(self.parts) - 1
        kernel = (second_kernel, third_kernel)[stage - 1]
        (send,) = self.line.call(
            functools.partial(kernel, self.order, self.stride),
            [(keep.shape[stage:], keep.dtype)],
            *self.parts,
            weight=STEP_WEIGHT,
        )
        self.parts.append(hop(send, self.order[stage], self.stride))


def total_kernel(order, stride, parts, total_ref):
    total_ref[...] = gathered(order, stride, *parts)


def scatter_rest(line, chunk, rows):
    (total,) = line.call(
        functools.partial(total_kernel, chunk.order, chunk.stride),
        [(chunk.parts[3].shape, F32)],
        chunk.parts,
        far=1,
    )
    size, stride = lax.axis_size("dp"), chunk.stride
    groups = [[g * stride + i for i in range(stride)] for g in range(size // stride)]

    def scatter(values, dimension):
        return near(
            lax.psum_scatter(
                values, "dp", scatter_dimension=dimension, axis_index_groups=groups, tiled=True
            )
        )

    if total.shape[0] == rows:
        return [scatter(total, 0)]
    return [scatter(total[:rows], 0), scatter(total[rows : rows + 4, :rows], 1)]


def shards(
    tower_input,
    patch_order,
    visible_count,
    joint_cotangent,
    mixer_in_copy,
    mixer_in_master,
    mixer_in_moment,
    mixer_in_average,
    mixer_out_copy,
    mixer_out_master,
    mixer_out_moment,
    mixer_out_average,
    expand_copy,
    expand_master,
    expand_moment,
    expand_average,
    contract_copy,
    contract_master,
    contract_moment,
    contract_average,
    norm_params_copy,
    norm_params_master,
    norm_params_moment,
    norm_params_average,
):
    seq_count, length, width = tower_input.shape[1:]
    inner = mixer_in_copy.shape[3]
    heads = inner // HD
    hidden_width = expand_copy.shape[2]
    dp_size = lax.axis_size("dp")
    stride = dp_size // SPLIT
    tower = lax.axis_index("tower")
    line = Line()
    act = (length, width)
    tokens = seq_count * length

    front_outs = [
        (act, BF),
        (act, BF),
        ((3, length, inner), BF),
        ((heads, length, length), BF),
        ((length, inner), BF),
    ]
    lead_far = [
        patch_order,
        visible_count,
        tower_input[0],
        jnp.transpose(mixer_in_copy[0], (1, 0, 2)),
        norm_params_copy[0],
        mixer_out_copy[0],
        joint_cotangent.reshape(2, length, width),
    ]
    lead = line.call(
        lead_kernel,
        [(v.shape, v.dtype) for v in lead_far] + [(act, BF), (act, BF)] + front_outs,
        *lead_far,
        raw=len(lead_far),
        scratch=[pltpu.SemaphoreType.DMA((len(lead_far),))],
    )
    patch_order, visible_count, x, w_in, norms, w_out, cot, att_zero, cot_send, *front_zero = lead
    att_zero_other = swap(att_zero, "mp")
    cot_other = swap(cot_send, "tower")
    next_far = [expand_copy[0], contract_copy[0]]
    w_up, w_down, att_one, *front_one = line.call(
        next_kernel,
        [(v.shape, v.dtype) for v in next_far] + [(act, BF)] + front_outs,
        *next_far,
        patch_order,
        visible_count,
        x,
        w_in,
        norms,
        w_out,
        raw=len(next_far),
        scratch=[pltpu.SemaphoreType.DMA((len(next_far),))],
    )
    att_one_other = swap(att_one, "mp")
    rows, firsts, qkvs, probs, ctxs = zip(front_zero, front_one)
    mids, backs_other = [], []
    for seq, pieces in enumerate(((att_zero, att_zero_other), (att_one, att_one_other))):
        mids.append(
            line.call(
                functools.partial(mid_kernel, seq),
                [
                    (act, BF),
                    (act, BF),
                    (act, F32),
                    (act, BF),
                    (act, BF),
                    ((length, hidden_width), BF),
                    ((length, hidden_width), BF),
                ],
                visible_count,
                rows[seq],
                *pieces,
                norms,
                w_up,
                w_down,
                cot,
                cot_other,
            )
        )
        backs_other.append(swap(mids[-1][0], "mp"))
    backs, outs, middles, seconds, finals, hiddens, pres = zip(*mids)

    order_a, order_b = (0, 1, 2), (1, 0, 2)

    orders = (order_a, order_b)
    def whole(lefts, rights, order):
        keep, send = line.call(
            functools.partial(grads_kernel, order, stride),
            [((2, 2, width // SPLIT, hidden_width), BF)] * 2,
            list(lefts),
            list(rights),
            scratch=[pltpu.VMEM((2, width // 2, tokens), BF)],
        )
        return [Chunk(line, keep, send, order, stride)]

    lasts = []

    def back(seq):
        lasts.append(
            line.call(
                back_kernel,
                [(act, BF), (act, BF), ((3, length, inner), BF), ((8, width), F32)],
                backs[seq],
                backs_other[seq],
                middles[seq],
                finals[seq],
                norms,
                w_out,
                w_in,
                qkvs[seq],
                probs[seq],
                rows[seq],
                lasts[0][3] if seq else None,
                scratch=[pltpu.VMEM((length, inner), BF)],
            )
        )

    def step(pair):
        for chunk in pair:
            chunk.step()

    rate_scale = 1.0 / math.sqrt(seq_count * dp_size * length)

    def update(parts, weights, indices):
        sizes = [g[0].shape for g in weights]
        lists = [c.parts for c in parts]
        if stride > 1:
            lists = [scatter_rest(line, c, width // SPLIT) for c in parts]
        values = line.call(
            functools.partial(
                update_kernel,
                [STEP_RATES[i] * rate_scale for i in indices],
                [c.order for c in parts],
                stride,
            ),
            [(s, F32 if i < 4 else BF) for s in sizes for i in range(5)],
            lists,
            *[[g[i] for g in weights] for i in range(3)],
            far=5 * len(weights),
            weight=STEP_WEIGHT,
        )
        return [values[5 * i : 5 * i + 5] for i in range(len(weights))]

    far_masters = [
        *[jnp.transpose(v[0], (1, 0, 2)) for v in (mixer_in_master, mixer_in_moment, mixer_in_average)],
        *[v[0].T for v in (mixer_out_master, mixer_out_moment, mixer_out_average)],
        *[v[0] for v in (norm_params_master, norm_params_moment, norm_params_average)],
        *[v[0] for v in (expand_master, expand_moment, expand_average)],
        *[v[0].T for v in (contract_master, contract_moment, contract_average)],
    ]

    down = whole(finals, hiddens, order_a)
    up = whole(seconds, pres, order_b)
    back(0)
    back(1)
    grad_firsts, grad_mids, mixeds, _ = zip(*lasts)
    norm_own = lasts[1][3]
    norm_other = swap(norm_own, "mp")
    both = ((seq_count,) + act, BF)
    keep_a, send_a, out_both, first_both = line.call(
        functools.partial(mixer_a_kernel, order_a, stride),
        [((2, 2, width // SPLIT + 8, width), BF)] * 2 + [both, both],
        list(firsts),
        list(mixeds),
        norm_own,
        norm_other,
        list(outs),
        list(grad_firsts),
        scratch=[pltpu.VMEM((2, width // 2, tokens), BF)],
    )
    first_other = swap(first_both, "mp")
    out_other = swap(out_both, "mp")
    mixer = [Chunk(line, keep_a, send_a, order_a, stride)]
    masters = line.call(
        fetch_kernel,
        [(v.shape, v.dtype) for v in far_masters],
        *far_masters,
        raw=len(far_masters),
        scratch=[pltpu.SemaphoreType.DMA((len(far_masters),))],
    )
    step(down)
    step(up)
    keep_b, send_b = line.call(
        functools.partial(mixer_b_kernel, order_b, stride),
        [((2, 2, width // SPLIT, width), BF)] * 2,
        list(grad_mids),
        list(ctxs),
        list(firsts),
        list(mixeds),
        scratch=[pltpu.VMEM((2, width // 2, tokens), BF)] * 2,
    )
    mixer.append(Chunk(line, keep_b, send_b, order_b, stride))
    (input_grad,) = line.call(
        input_kernel,
        [((seq_count,) + act, BF)],
        patch_order,
        visible_count,
        first_both,
        first_other,
        list(rows),
        list(grad_mids),
        norms,
        far=1,
    )
    step(down)
    step(mixer[:1])
    row_keep, row_send = line.call(
        final_kernel,
        [(act, BF), (act, BF)],
        visible_count,
        list(middles),
        out_both,
        out_other,
    )
    row_other = swap(row_send, "tower")
    step(up)
    step(mixer[1:])
    (down_set,) = update(down, [masters[12:15]], (3,))
    step(mixer[:1])
    step(mixer[1:])
    (joint_rows,) = line.call(
        join_kernel, [((2, length, width), BF)], row_keep, row_other, far=1
    )
    (up_set,) = update(up, [masters[9:12]], (2,))
    in_set, out_set, norm_set = update(mixer, [masters[0:3], masters[3:6], masters[6:9]], (0, 1, 4))
    return (
        joint_rows.reshape(1, 1, 2, seq_count // 2, length, width),
        input_grad[None],
        *[jnp.transpose(v, (1, 0, 2))[None] for v in in_set],
        *[v.T[None] for v in out_set],
        *[v[None] for v in up_set],
        *[v.T[None] for v in down_set],
        *[v[None] for v in norm_set],
    )


def solution(mesh):
    weight_in = P("tower", "dp", None, "mp")
    weight_out = P("tower", "mp", "dp")
    weight_up = P("tower", "dp", "mp")
    norm = P("tower", None, "dp")
    return jax.shard_map(
        shards,
        mesh=mesh,
        in_specs=(
            P("tower", "dp", None, None),
            P("dp", None),
            P("tower", "dp"),
            P("dp", "tower", None, None, None, None),
            P("tower", None, None, "mp"),
            *[weight_in] * 3,
            P("tower", "mp", None),
            *[weight_out] * 3,
            P("tower", None, "mp"),
            *[weight_up] * 3,
            P("tower", "mp", None),
            *[weight_out] * 3,
            P("tower", None, None),
            *[norm] * 3,
        ),
        out_specs=(
            P("dp", "tower", None, None, None, None),
            P("tower", "dp", None, None),
            *[weight_in] * 5,
            *[weight_out] * 5,
            *[weight_up] * 5,
            *[weight_out] * 5,
            *[norm] * 5,
        ),
        check_vma=False,
    )
```

```python
import functools
import math

import jax
import jax.numpy as jnp
from jax import lax
from jax.experimental import pallas as pl
from jax.experimental.pallas import tpu as pltpu
from jax.sharding import PartitionSpec as P

HD = 64
PAIR = 2 * HD
EPSILON = 1e-06
MOMENTUM = 0.9
AVERAGE_RATE = 0.6
STEP_RATES = (0.013, 1.3, 0.06, 0.015, 0.04)
SPLIT = 8
MICROSECOND = 1153500000
A_ORDER, B_ORDER = (0, 1, 2), (1, 0, 2)
GROUPS = ((0, 0, 6, A_ORDER), (1, 0, 6, B_ORDER))
PLAN = (
    ("lead", 2),
    ("next", 20),
    ("mid0", 12),
    ("mid1", 3),
    ("kC0", 0),
    ("sides", 3),
    ("kC1", 5),
    ("back0", 3),
    ("back1", 2),
    ("kM0", 1),
    ("s2C0", 3),
    ("cpA2", 0),
    ("kM1", 0.5),
    ("s2C1", 1),
    ("s2M0", 3),
    ("s3C0", 1),
    ("s3C1", 3),
    ("cpA4", 0),
    ("fin", 12),
    ("fetch", 40),
    ("s3M0", 12),
    ("s2M1", 12),
    ("join", 20),
    ("updC", 20),
    ("updE", 20),
    ("s3M1", 8),
    ("inp", 3),
    ("updM", 5),
)
BF = jnp.bfloat16
F32 = jnp.float32
VMEM_BYTES = 8 * 1024 * 1024


def dot(left, right):
    return lax.dot_general(left, right, (((1,), (0,)), ((), ())), preferred_element_type=F32)


def dot_t(left, right):
    return lax.dot_general(left, right, (((1,), (1,)), ((), ())), preferred_element_type=F32)


def t_dot(left, right):
    return lax.dot_general(left, right, (((0,), (0,)), ((), ())), preferred_element_type=F32)


def unit_and_scale(rows):
    centred = rows - jnp.mean(rows, axis=-1, keepdims=True)
    spread = jnp.mean(centred * centred, axis=-1, keepdims=True)
    scale = lax.rsqrt(spread + EPSILON)
    return centred * scale, scale


def norm_back(grad_out, unit, scale, gain):
    grad_unit = grad_out * gain
    inner = jnp.mean(grad_unit, axis=-1, keepdims=True)
    along = jnp.mean(grad_unit * unit, axis=-1, keepdims=True)
    return scale * (grad_unit - inner - unit * along)


def half_masks():
    lane = lax.broadcasted_iota(jnp.int32, (1, PAIR), 1)
    return [jnp.where(lane < HD, 1.0, 0.0).astype(BF), jnp.where(lane < HD, 0.0, 1.0).astype(BF)]


def place_table(order_ref, count, seq, length):
    slot = lax.broadcasted_iota(jnp.int32, (length, length), 0)
    lane = lax.broadcasted_iota(jnp.int32, (length, length), 1)
    own = jnp.where(lax.axis_index("tower") == 0, order_ref[seq : seq + 1, :], lane[0:1, :])
    return jnp.where((slot == own) & (lane < count), 1.0, 0.0).astype(BF)


def front_kernel(
    seq,
    order_ref,
    count_ref,
    x_ref,
    win_ref,
    norm_ref,
    rows_ref,
    first_ref,
    qkv_ref,
    probs_ref,
    ctx_ref,
    waits=(),
):
    length = x_ref.shape[1]
    inner = win_ref.shape[2]
    hold(waits, 0)
    count = count_ref[0:1, seq : seq + 1]
    table = place_table(order_ref, count, seq, length)
    rows = t_dot(table, x_ref[seq])
    rows_ref[...] = rows.astype(BF)
    unit, _ = unit_and_scale(rows)
    norms = norm_ref[...].astype(F32)
    first = (unit * norms[0:1] + norms[1:2]).astype(BF)
    first_ref[...] = first
    for part in range(3):
        hold(waits, 1 + part)
        qkv_ref[part] = dot(first, win_ref[part]).astype(BF)
    masks = half_masks()
    key_lane = lax.broadcasted_iota(jnp.int32, (1, length), 1) < count
    for pair in range(inner // PAIR):
        cols = pl.ds(pair * PAIR, PAIR)
        queries = qkv_ref[0, :, cols]
        keys = qkv_ref[1, :, cols]
        values = qkv_ref[2, :, cols]
        probs = []
        for half in range(2):
            scores = dot_t(queries * (masks[half] * HD**-0.5).astype(BF), keys)
            scores = jnp.where(key_lane, scores, -1e30)
            top = jnp.max(scores, axis=-1, keepdims=True)
            powers = jnp.exp(scores - top)
            total = jnp.sum(powers, axis=-1, keepdims=True)
            low = (powers * (1.0 / total)).astype(BF)
            probs_ref[2 * pair + half] = low
            probs.append(low)
        stacked = jnp.concatenate([values * masks[0], values * masks[1]], axis=0)
        ctx_ref[:, cols] = dot(jnp.concatenate(probs, axis=1), stacked).astype(BF)


def hold(waits, place):
    for copy in waits[place] if waits else ():
        copy.wait()


def begin(pairs, sems):
    copies = [
        pltpu.make_async_copy(source, target, sems.at[i])
        for i, (source, target) in enumerate(pairs)
    ]
    for copy in copies:
        copy.start()
    return copies


def row_pairs(source, target, parts):
    rows = source.shape[0] // parts
    cuts = [pl.ds(i * rows, rows) for i in range(parts)]
    return [(source.at[cut], target.at[cut]) for cut in cuts]


def attend(ctx_ref, wout_ref, att_ref):
    att_ref[...] = dot(ctx_ref[...], wout_ref[...]).astype(BF)


def lead_kernel(*refs):
    far, close, refs = refs[:7], refs[7:14], refs[14:]
    att_ref, cot_send_ref, *rest, sems = refs
    pairs = [(far[i], close[i]) for i in (0, 1, 4)]
    pairs += row_pairs(far[2].at[0], close[2].at[0], 2)
    for part in range(3):
        pairs += row_pairs(far[3].at[part], close[3].at[part], 2)
    pairs += row_pairs(far[5], close[5], 2)
    for seq in range(2):
        pairs += row_pairs(far[6].at[seq], close[6].at[seq], 1)
    pairs += row_pairs(far[2].at[1], close[2].at[1], 1)
    copies = begin(pairs, sems)
    waits = [copies[0:5], copies[5:7], copies[7:9], copies[9:11]]
    front_kernel(0, *close[:5], *rest, waits=waits)
    for copy in copies[11:13]:
        copy.wait()
    attend(rest[-1], close[5], att_ref)
    for copy in copies[13:]:
        copy.wait()
    cot_send_ref[...] = close[6][1 - lax.axis_index("tower")]


def next_kernel(*refs):
    far, ins, close, refs = refs[:2], refs[2:8], refs[8:10], refs[10:]
    att_ref, *rest, sems = refs
    copies = begin(row_pairs(far[0], close[0], 4) + row_pairs(far[1], close[1], 4), sems)
    front_kernel(1, *ins[:5], *rest)
    attend(rest[-1], ins[5], att_ref)
    for copy in copies:
        copy.wait()


def fetch_kernel(*refs):
    count = len(refs) // 2
    for copy in begin(zip(refs[:count], refs[count : 2 * count]), refs[-1]):
        copy.wait()


def mid_kernel(
    seq,
    count_ref,
    rows_ref,
    att_ref,
    att_other_ref,
    norm_ref,
    wup_ref,
    wdown_ref,
    cot_ref,
    cot_other_ref,
    middle_ref,
    second_ref,
    final_ref,
    hidden_ref,
    pre_ref,
):
    length = rows_ref.shape[0]
    hidden_width = wup_ref.shape[1]
    attended = att_ref[...].astype(F32) + att_other_ref[...].astype(F32)
    middle = rows_ref[...].astype(F32) + attended
    middle_ref[...] = middle
    unit, _ = unit_and_scale(middle)
    norms = norm_ref[...].astype(F32)
    second = (unit * norms[2:3] + norms[3:4]).astype(BF)
    second_ref[...] = second
    valid = lax.broadcasted_iota(jnp.int32, (length, 1), 0) < count_ref[0:1, seq : seq + 1]
    cot = jnp.where(lax.axis_index("tower") == seq, cot_ref[seq], cot_other_ref[...])
    grad_final = jnp.where(valid, cot.astype(F32), 0.0).astype(BF)
    final_ref[...] = grad_final
    tile = 256
    for step in range(hidden_width // tile):
        cols = pl.ds(step * tile, tile)
        pre = dot(second, wup_ref[:, cols])
        grad_hidden = dot_t(grad_final, wdown_ref[cols, :])
        power = jnp.exp(pre * pre * -0.5)
        reach = 1.0 / (1.0 + jnp.abs(pre) * (0.3275911 / math.sqrt(2.0)))
        tail = (
            reach
            * (
                0.127414796
                + reach
                * (
                    -0.142248368
                    + reach * (0.7107068705 + reach * (-0.7265760135 + reach * 0.5307027145))
                )
            )
            * power
        )
        phi = jnp.where(pre >= 0.0, 1.0 - tail, tail)
        hidden_ref[:, cols] = (pre * phi).astype(BF)
        slope = phi + pre * (power * (1.0 / math.sqrt(2.0 * math.pi)))
        pre_ref[:, cols] = (grad_hidden * slope).astype(BF)


def sides_kernel(wup_ref, wdown_ref, hidden_ref, pre_ref, back_ref, out_ref):
    back_ref[...] = dot_t(pre_ref[...], wup_ref[...]).astype(BF)
    out_ref[...] = dot(hidden_ref[...], wdown_ref[...]).astype(BF)


def whole_mid_kernel(seq, *refs):
    mid_kernel(seq, *refs[:9], *refs[11:])
    sides_kernel(refs[5], refs[6], *refs[14:16], *refs[9:11])


def block_home(own, block, order):
    which = 1 - ((block >> order[0]) & 1) if own else (block >> order[0]) & 1
    return which, 2 * ((block >> order[1]) & 1) + ((block >> order[2]) & 1)


def store_blocks(order, stride, left, left_scr):
    rows = left.shape[0] // SPLIT
    own = (lax.axis_index("dp") // (stride << order[0])) & 1
    for side in range(2):

        @pl.when(own == side)
        def _():
            for block in range(SPLIT):
                which, place = block_home(side, block, order)
                left_scr[which, place * rows : (place + 1) * rows, :] = left[
                    block * rows : (block + 1) * rows
                ]


def grads_kernel(order, stride, cols, lefts, rights, keep_ref, send_ref, left_scr):
    store_blocks(order, stride, jnp.concatenate([r[...].T for r in lefts], axis=1), left_scr)
    right = jnp.concatenate([r[:, cols] for r in rights], axis=0)
    send_ref[...] = dot(left_scr[1], right).astype(BF).reshape(send_ref.shape)
    keep_ref[...] = dot(left_scr[0], right).astype(BF).reshape(keep_ref.shape)


def copy_kernel(sources, target_ref):
    for place, source in enumerate(sources):
        target_ref[place] = source[...]


def mixer_a_kernel(
    order,
    stride,
    first_refs,
    mixed_refs,
    norm_own_ref,
    norm_other_ref,
    keep_ref,
    send_ref,
    first_scr,
):
    inner = mixed_refs[0].shape[2]
    store_blocks(order, stride, jnp.concatenate([r[...].T for r in first_refs], axis=1), first_scr)
    rows = first_scr.shape[1] // 4
    shape = (2, 2, rows, inner)
    mixed = [jnp.concatenate([r[part] for r in mixed_refs], axis=0) for part in range(2)]
    for which, ref in ((1, send_ref), (0, keep_ref)):
        for part in range(2):
            cols = slice(part * inner, (part + 1) * inner)
            ref[:, :, 0:rows, cols] = dot(first_scr[which], mixed[part]).astype(BF).reshape(shape)
        ref[:, :, rows:, :] = jnp.zeros((2, 2, 8, 2 * inner), BF)
    own_norm = norm_own_ref[...]
    row = lax.broadcasted_iota(jnp.int32, (8, 1), 0)
    norm_grad = own_norm + jnp.where(row < 2, norm_other_ref[...], 0.0)
    own = own_bit(order, 0, stride)
    for block in range(SPLIT):
        piece = norm_grad[:, block * rows : (block + 1) * rows].astype(BF)
        bits = [(block >> o) & 1 for o in order]

        @pl.when(own == bits[0])
        def _():
            keep_ref[bits[1], bits[2], rows:, 0:rows] = piece

        @pl.when(own != bits[0])
        def _():
            send_ref[bits[1], bits[2], rows:, 0:rows] = piece


def mixer_b_kernel(
    order,
    stride,
    mid_refs,
    ctx_refs,
    first_refs,
    mixed_refs,
    keep_ref,
    send_ref,
    first_scr,
    mid_scr,
):
    inner = ctx_refs[0].shape[1]
    store_blocks(order, stride, jnp.concatenate([r[...].T for r in first_refs], axis=1), first_scr)
    store_blocks(order, stride, jnp.concatenate([r[...].T for r in mid_refs], axis=1), mid_scr)
    right = jnp.concatenate([r[...] for r in ctx_refs], axis=0)
    mixed = jnp.concatenate([r[2] for r in mixed_refs], axis=0)
    shape = keep_ref.shape[:3] + (inner,)
    for which, ref in ((1, send_ref), (0, keep_ref)):
        ref[:, :, :, 0:inner] = dot(first_scr[which], mixed).astype(BF).reshape(shape)
        ref[:, :, :, inner : 2 * inner] = dot(mid_scr[which], right).astype(BF).reshape(shape)


def back_kernel(
    own_ref,
    other_ref,
    middle_ref,
    final_ref,
    norm_ref,
    wout_ref,
    win_ref,
    qkv_ref,
    probs_ref,
    rows_ref,
    before_ref,
    first_ref,
    mid_ref,
    mixed_ref,
    norm_grad_ref,
    ctx_grad_scr,
):
    inner = wout_ref.shape[0]
    grad_second = own_ref[...].astype(F32) + other_ref[...].astype(F32)
    unit, scale = unit_and_scale(middle_ref[...])
    second_gain = jnp.sum(grad_second * unit, axis=0, keepdims=True)
    second_shift = jnp.sum(grad_second, axis=0, keepdims=True)
    gain = norm_ref[2:3].astype(F32)
    grad_mid = final_ref[...].astype(F32) + norm_back(grad_second, unit, scale, gain)
    grad_mid = grad_mid.astype(BF)
    mid_ref[...] = grad_mid
    ctx_grad_scr[...] = dot_t(grad_mid, wout_ref[...]).astype(BF)
    masks = half_masks()
    for pair in range(inner // PAIR):
        cols = pl.ds(pair * PAIR, PAIR)
        queries = qkv_ref[0, :, cols]
        keys = qkv_ref[1, :, cols]
        values = qkv_ref[2, :, cols]
        grad_ctx = ctx_grad_scr[:, cols]
        halves = [grad_ctx * masks[0], grad_ctx * masks[1]]
        probs, slopes = [], []
        for half in range(2):
            low = probs_ref[2 * pair + half]
            prob = low.astype(F32)
            grad_probs = dot_t(halves[half], values)
            along = jnp.sum(prob * grad_probs, axis=-1, keepdims=True)
            slopes.append((prob * (grad_probs - along)).astype(BF))
            probs.append(low)
        key_stack = jnp.concatenate([keys * masks[0], keys * masks[1]], axis=0)
        query_stack = jnp.concatenate([queries * masks[0], queries * masks[1]], axis=0)
        grad_q = dot(jnp.concatenate(slopes, axis=1), key_stack) * HD**-0.5
        grad_k = t_dot(jnp.concatenate(slopes, axis=0), query_stack) * HD**-0.5
        grad_v = t_dot(jnp.concatenate(probs, axis=0), jnp.concatenate(halves, axis=0))
        mixed_ref[0, :, cols] = grad_q.astype(BF)
        mixed_ref[1, :, cols] = grad_k.astype(BF)
        mixed_ref[2, :, cols] = grad_v.astype(BF)
    total = dot_t(mixed_ref[0], win_ref[0])
    for part in range(1, 3):
        total += dot_t(mixed_ref[part], win_ref[part])
    first_ref[...] = total.astype(BF)
    unit, _ = unit_and_scale(rows_ref[...].astype(F32))
    norm_grad = jnp.concatenate(
        [
            jnp.sum(total * unit, axis=0, keepdims=True),
            jnp.sum(total, axis=0, keepdims=True),
            second_gain,
            second_shift,
            jnp.zeros((4, total.shape[1]), F32),
        ],
        axis=0,
    )
    norm_grad_ref[...] = norm_grad if before_ref is None else norm_grad + before_ref[...]


def input_kernel(
    order_ref, count_ref, own_ref, other_ref, rows_refs, mid_refs, norm_ref, out_ref
):
    length = rows_refs[0].shape[0]
    gain = norm_ref[0:1].astype(F32)
    for seq in range(len(rows_refs)):
        grad_first = own_ref[seq].astype(F32) + other_ref[seq].astype(F32)
        unit, scale = unit_and_scale(rows_refs[seq][...].astype(F32))
        grad_rows = mid_refs[seq][...].astype(F32) + norm_back(grad_first, unit, scale, gain)
        table = place_table(order_ref, count_ref[0:1, seq : seq + 1], seq, length)
        out_ref[seq] = dot(table, grad_rows.astype(BF)).astype(BF)


def final_kernel(count_ref, middle_refs, own_ref, other_ref, keep_ref, send_ref):
    length = middle_refs[0].shape[0]
    row = lax.broadcasted_iota(jnp.int32, (length, 1), 0)
    tower = lax.axis_index("tower")
    for seq in range(2):
        output = own_ref[seq].astype(F32) + other_ref[seq].astype(F32)
        final = jnp.where(row < count_ref[0:1, seq : seq + 1], middle_refs[seq][...] + output, 0.0).astype(BF)

        @pl.when(tower == seq)
        def _():
            keep_ref[...] = final

        @pl.when(tower != seq)
        def _():
            send_ref[...] = final


def join_kernel(keep_ref, other_ref, out_ref):
    tower = lax.axis_index("tower")
    out_ref[tower] = keep_ref[...]
    out_ref[1 - tower] = other_ref[...]


def update_values(gradient, master, moment, average, rate):
    moment_new = MOMENTUM * moment + gradient
    master_new = master - rate * (gradient + MOMENTUM * moment_new)
    average_new = AVERAGE_RATE * average + (1.0 - AVERAGE_RATE) * master_new
    return gradient, master_new, moment_new, average_new, master_new.astype(BF)


def update_kernel(rates, stride, groups, masters, moments, averages, *outs):
    total, norm_total = {}, None
    for place, chunks in enumerate(groups):
        rows = masters[place].shape[-2]
        pieces = []
        for order, parts in chunks:
            piece = gathered(order, stride, *parts) if len(parts) == 4 else parts[0][...]
            if len(parts) == 2:
                norm_total = parts[1][...]
            if piece.shape[0] > rows:
                norm_total = piece[rows : rows + 4, 0:rows]
            pieces.append(piece[0:rows])
        total[place] = jnp.concatenate(pieces, axis=1)
    first, start = total[0], 0
    for place, rate in enumerate(rates):
        group = outs[5 * place : 5 * place + 5]
        deep = masters[place].ndim == 3
        columns = masters[place].shape[-1]
        for piece in range(masters[place].shape[0] if deep else 1):
            at = piece if deep else Ellipsis
            if place == 2:
                gradient = norm_total
            elif place < len(groups):
                gradient = total[place][:, piece * columns : (piece + 1) * columns]
            else:
                gradient = first[:, start : start + columns]
            if place == 0:
                start += columns
            values = update_values(
                gradient, masters[place][at], moments[place][at], averages[place][at], rate
            )
            for ref, value in zip(group, values):
                ref[at] = value


def near(values):
    return pltpu.with_memory_space_constraint(values, pltpu.VMEM)


class Line:
    def __init__(self):
        self.token = None
        self.weight = 0

    def call(self, kernel, outs, *args, far=0, raw=0, scratch=()):
        flat, tree = jax.tree.flatten(args)
        flat = [pltpu.with_memory_space_constraint(v, pltpu.HBM) for v in flat[:raw]] + flat[raw:]
        extra = [] if self.token is None else [self.token]
        near_outs = [pltpu.VMEM(s, d) for s, d in outs[far:]]
        far_outs = [jax.ShapeDtypeStruct(s, d) for s, d in outs[:far]]
        count, gap = len(flat), len(extra)

        def body(*refs):
            ins = jax.tree.unflatten(tree, refs[:count])
            rest = refs[count + gap :]
            kernel(*ins, *rest[: len(outs)], *rest[len(outs) + 1 :])
            rest[len(outs)][...] = jnp.zeros((8, 128), F32)

        whole = pl.BlockSpec(memory_space=pltpu.VMEM)
        *results, self.token = pl.pallas_call(
            body,
            out_shape=far_outs + near_outs + [pltpu.VMEM((8, 128), F32)],
            in_specs=[pl.BlockSpec(memory_space=pltpu.HBM)] * raw + [whole] * (count + gap - raw),
            out_specs=[whole] * (len(outs) + 1),
            scratch_shapes=list(scratch),
            compiler_params=pltpu.CompilerParams(vmem_limit_bytes=VMEM_BYTES),
            cost_estimate=pl.CostEstimate(
                flops=int(self.weight * MICROSECOND), transcendentals=0, bytes_accessed=0
            ),
        )(*flat, *extra)
        return results


def swap(values, axis):
    return near(lax.ppermute(values, axis, [(0, 1), (1, 0)]))


def hop(values, bit, stride):
    size = lax.axis_size("dp")
    step = stride << bit
    return near(lax.ppermute(values, "dp", [(i, i ^ step) for i in range(size)]))


def own_bit(order, stage, stride):
    return (lax.axis_index("dp") // (stride << order[stage])) & 1


def second_kernel(order, stride, keep_ref, one_ref, send_ref):
    other = 1 - own_bit(order, 1, stride)
    total = keep_ref[other].astype(F32) + one_ref[other].astype(F32)
    send_ref[...] = total.astype(send_ref.dtype)


def third_kernel(order, stride, keep_ref, one_ref, two_ref, send_ref):
    own = own_bit(order, 1, stride)
    other = 1 - own_bit(order, 2, stride)
    total = keep_ref[own, other].astype(F32) + one_ref[own, other].astype(F32)
    send_ref[...] = (total + two_ref[other].astype(F32)).astype(send_ref.dtype)


def gathered(order, stride, keep_ref, one_ref, two_ref, three_ref):
    two, three = own_bit(order, 1, stride), own_bit(order, 2, stride)
    total = keep_ref[two, three].astype(F32) + one_ref[two, three].astype(F32)
    return total + two_ref[three].astype(F32) + three_ref[...].astype(F32)


class Chunk:
    def __init__(self, line, keep, send, order, stride):
        self.line, self.order, self.stride = line, order, stride
        self.parts = [keep, hop(send, order[0], stride)]

    def step(self):
        keep = self.parts[0]
        stage = len(self.parts) - 1
        kernel = (second_kernel, third_kernel)[stage - 1]
        (send,) = self.line.call(
            functools.partial(kernel, self.order, self.stride),
            [(keep.shape[stage:], keep.dtype)],
            *self.parts,
        )
        self.parts.append(hop(send, self.order[stage], self.stride))


def total_kernel(order, stride, parts, total_ref):
    total_ref[...] = gathered(order, stride, *parts)


def scatter_rest(line, chunk, rows):
    (total,) = line.call(
        functools.partial(total_kernel, chunk.order, chunk.stride),
        [(chunk.parts[3].shape, F32)],
        chunk.parts,
        far=1,
    )
    size, stride = lax.axis_size("dp"), chunk.stride
    groups = [[g * stride + i for i in range(stride)] for g in range(size // stride)]

    def scatter(values, dimension):
        return near(
            lax.psum_scatter(
                values, "dp", scatter_dimension=dimension, axis_index_groups=groups, tiled=True
            )
        )

    if total.shape[0] == rows:
        return [scatter(total, 0)]
    return [scatter(total[:rows], 0), scatter(total[rows : rows + 4, :rows], 1)]


def shards(
    tower_input,
    patch_order,
    visible_count,
    joint_cotangent,
    mixer_in_copy,
    mixer_in_master,
    mixer_in_moment,
    mixer_in_average,
    mixer_out_copy,
    mixer_out_master,
    mixer_out_moment,
    mixer_out_average,
    expand_copy,
    expand_master,
    expand_moment,
    expand_average,
    contract_copy,
    contract_master,
    contract_moment,
    contract_average,
    norm_params_copy,
    norm_params_master,
    norm_params_moment,
    norm_params_average,
):
    seq_count, length, width = tower_input.shape[1:]
    inner = mixer_in_copy.shape[3]
    heads = inner // HD
    hidden_width = expand_copy.shape[2]
    dp_size = lax.axis_size("dp")
    stride = dp_size // SPLIT
    tower = lax.axis_index("tower")
    line = Line()
    act = (length, width)
    both = ((seq_count,) + act, BF)
    tokens = seq_count * length
    left_scratch = pltpu.VMEM((2, width // 2, tokens), BF)
    front_outs = [
        (act, BF),
        (act, BF),
        ((3, length, inner), BF),
        ((heads, length, length), BF),
        ((length, inner), BF),
    ]
    got, chunks = {}, {}

    def lead():
        far = [
            patch_order,
            visible_count,
            tower_input[0],
            jnp.transpose(mixer_in_copy[0], (1, 0, 2)),
            norm_params_copy[0],
            mixer_out_copy[0],
            joint_cotangent.reshape(2, length, width),
        ]
        results = line.call(
            lead_kernel,
            [(v.shape, v.dtype) for v in far] + [(act, BF), (act, BF)] + front_outs,
            *far,
            raw=len(far),
            scratch=[pltpu.SemaphoreType.DMA((16,))],
        )
        got["fixed"], got["att0"], got["front0"] = results[:7], results[7], results[9:]
        got["cot_other"] = swap(results[8], "tower")
        got["att0_other"] = swap(results[7], "mp")

    def following():
        far = [expand_copy[0], contract_copy[0]]
        w_up, w_down, att, *front = line.call(
            next_kernel,
            [(v.shape, v.dtype) for v in far] + [(act, BF)] + front_outs,
            *far,
            *got["fixed"][:6],
            raw=len(far),
            scratch=[pltpu.SemaphoreType.DMA((8,))],
        )
        got["wide"], got["att1"], got["front1"] = (w_up, w_down), att, front
        got["att1_other"] = swap(att, "mp")

    mid_outs = [
        (act, F32),
        (act, BF),
        (act, BF),
        ((length, hidden_width), BF),
        ((length, hidden_width), BF),
    ]

    def mid(seq):
        _, count, _, _, norms, _, cot = got["fixed"]
        kernel, outs = (mid_kernel, []) if seq else (whole_mid_kernel, [(act, BF)] * 2)
        results = line.call(
            functools.partial(kernel, seq),
            outs + mid_outs,
            count,
            got[f"front{seq}"][0],
            got[f"att{seq}"],
            got[f"att{seq}_other"],
            norms,
            *got["wide"],
            cot,
            got["cot_other"],
        )
        if seq:
            got["mid1"] = [None, None] + results
        else:
            got["mid0"] = results
            got["back_other0"] = swap(results[0], "mp")

    def sides():
        hidden, pre = got["mid1"][5:7]
        results = line.call(sides_kernel, [(act, BF)] * 2, *got["wide"], hidden, pre)
        got["mid1"][0:2] = results
        got["back_other1"] = swap(results[0], "mp")

    def pick(name, place):
        return [got[f"{name}{seq}"][place] for seq in range(2)]

    def group(index):
        source, start, stop, order = GROUPS[index]
        cols = slice(start * hidden_width // 6, stop * hidden_width // 6)
        columns = cols.stop - cols.start
        lefts, rights = ((4, 5), (3, 6))[source]
        keep, send = line.call(
            functools.partial(grads_kernel, order, stride, cols),
            [((2, 2, width // SPLIT, columns), BF)] * 2,
            pick("mid", lefts),
            pick("mid", rights),
            scratch=[left_scratch],
        )
        chunks[f"C{index}"] = Chunk(line, keep, send, order, stride)

    def back(seq):
        _, _, _, w_in, norms, w_out, _ = got["fixed"]
        rows, _, qkv, probs, _ = got[f"front{seq}"]
        first, _, middle, _, final, _, _ = got[f"mid{seq}"]
        got[f"last{seq}"] = line.call(
            back_kernel,
            [(act, BF), (act, BF), ((3, length, inner), BF), ((8, width), F32)],
            first,
            got[f"back_other{seq}"],
            middle,
            final,
            norms,
            w_out,
            w_in,
            qkv,
            probs,
            rows,
            got["last0"][3] if seq else None,
            scratch=[pltpu.VMEM((length, inner), BF)],
        )
        if seq:
            got["norm_other"] = swap(got["last1"][3], "mp")

    def share(name, sources):
        (result,) = line.call(copy_kernel, [both], sources)
        got[name], got[name + "_other"] = result, swap(result, "mp")

    def mixer_a():
        keep, send = line.call(
            functools.partial(mixer_a_kernel, A_ORDER, stride),
            [((2, 2, width // SPLIT + 8, 2 * inner), BF)] * 2,
            pick("front", 1),
            pick("last", 2),
            got["last1"][3],
            got["norm_other"],
            scratch=[left_scratch],
        )
        chunks["M0"] = Chunk(line, keep, send, A_ORDER, stride)

    def mixer_b():
        keep, send = line.call(
            functools.partial(mixer_b_kernel, B_ORDER, stride),
            [((2, 2, width // SPLIT, 2 * inner), BF)] * 2,
            pick("last", 1),
            pick("front", 4),
            pick("front", 1),
            pick("last", 2),
            scratch=[left_scratch] * 2,
        )
        chunks["M1"] = Chunk(line, keep, send, B_ORDER, stride)

    def fetch_masters():
        far = [
            *[jnp.transpose(v[0], (1, 0, 2)) for v in (mixer_in_master, mixer_in_moment, mixer_in_average)],
            *[v[0].T for v in (mixer_out_master, mixer_out_moment, mixer_out_average)],
            *[v[0] for v in (norm_params_master, norm_params_moment, norm_params_average)],
            *[v[0].T for v in (contract_master, contract_moment, contract_average)],
            *[v[0] for v in (expand_master, expand_moment, expand_average)],
        ]
        got["masters"] = line.call(
            fetch_kernel,
            [(v.shape, v.dtype) for v in far],
            *far,
            raw=len(far),
            scratch=[pltpu.SemaphoreType.DMA((len(far),))],
        )

    def input_side():
        patches, count, _, _, norms, _, _ = got["fixed"]
        (got["input_grad"],) = line.call(
            input_kernel,
            [both],
            patches,
            count,
            got["firsts"],
            got["firsts_other"],
            pick("front", 0),
            pick("last", 1),
            norms,
            far=1,
        )

    def final_side():
        got["keep"], send = line.call(
            final_kernel,
            [(act, BF), (act, BF)],
            got["fixed"][1],
            pick("mid", 2),
            got["outs"],
            got["outs_other"],
        )
        got["row_other"] = swap(send, "tower")

    def join():
        (got["joint"],) = line.call(
            join_kernel, [((2, length, width), BF)], got["keep"], got["row_other"], far=1
        )

    rate_scale = 1.0 / math.sqrt(seq_count * dp_size * length)

    def update(name, names, start, indices):
        lists = [[chunks[n] for n in group_names] for group_names in names]
        weights = [got["masters"][3 * i : 3 * i + 3] for i in range(start, start + len(indices))]
        sizes = [g[0].shape for g in weights]
        groups = []
        for members in lists:
            groups.append(
                [
                    (c.order, scatter_rest(line, c, width // SPLIT) if stride > 1 else c.parts)
                    for c in members
                ]
            )
        orders = [[order for order, _ in members] for members in groups]

        def kernel(parts, *refs):
            paired = [list(zip(o, p)) for o, p in zip(orders, parts)]
            update_kernel([STEP_RATES[i] * rate_scale for i in indices], stride, paired, *refs)

        values = line.call(
            kernel,
            [(s, F32 if i < 4 else BF) for s in sizes for i in range(5)],
            [[parts for _, parts in members] for members in groups],
            *[[g[i] for g in weights] for i in range(3)],
            far=5 * len(weights),
        )
        got[name] = [values[5 * i : 5 * i + 5] for i in range(len(weights))]

    def source_names(source):
        return [f"C{i}" for i, g in enumerate(GROUPS) if g[0] == source]

    steps = {
        "lead": lead,
        "next": following,
        "mid0": lambda: mid(0),
        "mid1": lambda: mid(1),
        "sides": sides,
        "back0": lambda: back(0),
        "back1": lambda: back(1),
        "cpA4": lambda: share("firsts", pick("last", 0)),
        "cpA2": lambda: share("outs", pick("mid", 1)),
        "fetch": fetch_masters,
        "kM0": mixer_a,
        "kM1": mixer_b,
        "inp": input_side,
        "fin": final_side,
        "join": join,
        "updC": lambda: update("down", [source_names(0)], 3, (3,)),
        "updE": lambda: update("up", [source_names(1)], 4, (2,)),
        "updM": lambda: update("mixer", [["M0", "M1"]], 0, (0, 1, 4)),
    }
    for name, weight in PLAN:
        line.weight = weight
        if name in steps:
            steps[name]()
        elif name.startswith("kC"):
            group(int(name[2:]))
        else:
            chunks[name[2:]].step()

    in_set, out_set, norm_set = got["mixer"]
    (down_set,), (up_set,) = got["down"], got["up"]
    return (
        got["joint"].reshape(1, 1, 2, seq_count // 2, length, width),
        got["input_grad"][None],
        *[jnp.transpose(v, (1, 0, 2))[None] for v in in_set],
        *[v.T[None] for v in out_set],
        *[v[None] for v in up_set],
        *[v.T[None] for v in down_set],
        *[v[None] for v in norm_set],
    )


def solution(mesh):
    weight_in = P("tower", "dp", None, "mp")
    weight_out = P("tower", "mp", "dp")
    weight_up = P("tower", "dp", "mp")
    norm = P("tower", None, "dp")
    return jax.shard_map(
        shards,
        mesh=mesh,
        in_specs=(
            P("tower", "dp", None, None),
            P("dp", None),
            P("tower", "dp"),
            P("dp", "tower", None, None, None, None),
            P("tower", None, None, "mp"),
            *[weight_in] * 3,
            P("tower", "mp", None),
            *[weight_out] * 3,
            P("tower", None, "mp"),
            *[weight_up] * 3,
            P("tower", "mp", None),
            *[weight_out] * 3,
            P("tower", None, None),
            *[norm] * 3,
        ),
        out_specs=(
            P("dp", "tower", None, None, None, None),
            P("tower", "dp", None, None),
            *[weight_in] * 5,
            *[weight_out] * 5,
            *[weight_up] * 5,
            *[weight_out] * 5,
            *[norm] * 5,
        ),
        check_vma=False,
    )
```

```python
import functools
import math

import jax
import jax.numpy as jnp
from jax import lax
from jax.experimental import pallas as pl
from jax.experimental.pallas import tpu as pltpu
from jax.sharding import PartitionSpec as P

HD = 64
PAIR = 2 * HD
EPSILON = 1e-06
MOMENTUM = 0.9
AVERAGE_RATE = 0.6
STEP_RATES = (0.013, 1.3, 0.06, 0.015, 0.04)
SPLIT = 8
MICROSECOND = 1153500000
A_ORDER, B_ORDER = (0, 1, 2), (1, 0, 2)
MIX_ORDER = A_ORDER
GROUPS = ((0, 0, 6, A_ORDER), (1, 0, 6, B_ORDER))
PLAN = (
    ("lead", 40),
    ("next", 40),
    ("mid0", 0),
    ("mid1", 20),
    ("kC0", 2),
    ("sides", 0.5),
    ("kC1", 1),
    ("hC1", 2),
    ("back0", 8),
    ("back1", 20),
    ("hC0", 0.5),
    ("s2C0", 3),
    ("kM0", 6),
    ("kM1", 0.5),
    ("s2C1", 5),
    ("cpA2", 0),
    ("s3C0", 8),
    ("s2M0", 1),
    ("fetch", 0.5),
    ("fin", 2),
    ("s3C1", 0),
    ("cpA4", 6),
    ("join", 6),
    ("updC", 8),
    ("s2M1", 3),
    ("s3M0", 4),
    ("updE", 3),
    ("s3M1", 6),
    ("inp", 0),
    ("updM", 1),
)
BF = jnp.bfloat16
F32 = jnp.float32
VMEM_BYTES = 8 * 1024 * 1024


def dot(left, right):
    return lax.dot_general(left, right, (((1,), (0,)), ((), ())), preferred_element_type=F32)


def dot_t(left, right):
    return lax.dot_general(left, right, (((1,), (1,)), ((), ())), preferred_element_type=F32)


def t_dot(left, right):
    return lax.dot_general(left, right, (((0,), (0,)), ((), ())), preferred_element_type=F32)


def unit_and_scale(rows):
    centred = rows - jnp.mean(rows, axis=-1, keepdims=True)
    spread = jnp.mean(centred * centred, axis=-1, keepdims=True)
    scale = lax.rsqrt(spread + EPSILON)
    return centred * scale, scale


def norm_back(grad_out, unit, scale, gain):
    grad_unit = grad_out * gain
    inner = jnp.mean(grad_unit, axis=-1, keepdims=True)
    along = jnp.mean(grad_unit * unit, axis=-1, keepdims=True)
    return scale * (grad_unit - inner - unit * along)


def half_masks():
    lane = lax.broadcasted_iota(jnp.int32, (1, PAIR), 1)
    return [jnp.where(lane < HD, 1.0, 0.0).astype(BF), jnp.where(lane < HD, 0.0, 1.0).astype(BF)]


def place_table(order_ref, count, seq, length):
    slot = lax.broadcasted_iota(jnp.int32, (length, length), 0)
    lane = lax.broadcasted_iota(jnp.int32, (length, length), 1)
    own = jnp.where(lax.axis_index("tower") == 0, order_ref[seq : seq + 1, :], lane[0:1, :])
    return jnp.where((slot == own) & (lane < count), 1.0, 0.0).astype(BF)


def front_kernel(
    seq,
    order_ref,
    count_ref,
    x_ref,
    win_ref,
    norm_ref,
    rows_ref,
    first_ref,
    qkv_ref,
    probs_ref,
    ctx_ref,
    waits=(),
):
    length = x_ref.shape[1]
    inner = win_ref.shape[2]
    hold(waits, 0)
    count = count_ref[0:1, seq : seq + 1]
    table = place_table(order_ref, count, seq, length)
    rows = t_dot(table, x_ref[seq])
    rows_ref[...] = rows.astype(BF)
    unit, _ = unit_and_scale(rows)
    norms = norm_ref[...].astype(F32)
    first = (unit * norms[0:1] + norms[1:2]).astype(BF)
    first_ref[...] = first
    for part in range(3):
        hold(waits, 1 + part)
        qkv_ref[part] = dot(first, win_ref[part]).astype(BF)
    masks = half_masks()
    key_lane = lax.broadcasted_iota(jnp.int32, (1, length), 1) < count
    pairs = [pl.ds(pair * PAIR, PAIR) for pair in range(inner // PAIR)]
    scores = []
    for cols in pairs:
        for half in range(2):
            queries = qkv_ref[0, :, cols] * (masks[half] * HD**-0.5).astype(BF)
            scores.append(jnp.where(key_lane, dot_t(queries, qkv_ref[1, :, cols]), -1e30))
    probs = []
    for head, score in enumerate(scores):
        powers = jnp.exp(score - jnp.max(score, axis=-1, keepdims=True))
        low = (powers * (1.0 / jnp.sum(powers, axis=-1, keepdims=True))).astype(BF)
        probs_ref[head] = low
        probs.append(low)
    for pair, cols in enumerate(pairs):
        values = qkv_ref[2, :, cols]
        stacked = jnp.concatenate([values * masks[0], values * masks[1]], axis=0)
        both = jnp.concatenate(probs[2 * pair : 2 * pair + 2], axis=1)
        ctx_ref[:, cols] = dot(both, stacked).astype(BF)


def hold(waits, place):
    for copy in waits[place] if waits else ():
        copy.wait()


def begin(pairs, sems):
    copies = [
        pltpu.make_async_copy(source, target, sems.at[i])
        for i, (source, target) in enumerate(pairs)
    ]
    for copy in copies:
        copy.start()
    return copies


def row_pairs(source, target, parts):
    rows = source.shape[0] // parts
    cuts = [pl.ds(i * rows, rows) for i in range(parts)]
    return [(source.at[cut], target.at[cut]) for cut in cuts]


def attend(ctx_ref, wout_ref, att_ref):
    att_ref[...] = dot(ctx_ref[...], wout_ref[...]).astype(BF)


def lead_kernel(*refs):
    far, close, refs = refs[:7], refs[7:14], refs[14:]
    att_ref, cot_send_ref, *rest, sems = refs
    pairs = [(far[i], close[i]) for i in (0, 1, 4)]
    pairs += row_pairs(far[2].at[0], close[2].at[0], 2)
    for part in range(3):
        pairs += row_pairs(far[3].at[part], close[3].at[part], 2)
    pairs += row_pairs(far[5], close[5], 2)
    for seq in range(2):
        pairs += row_pairs(far[6].at[seq], close[6].at[seq], 1)
    pairs += row_pairs(far[2].at[1], close[2].at[1], 1)
    copies = begin(pairs, sems)
    waits = [copies[0:5], copies[5:7], copies[7:9], copies[9:11]]
    front_kernel(0, *close[:5], *rest, waits=waits)
    for copy in copies[11:13]:
        copy.wait()
    attend(rest[-1], close[5], att_ref)
    for copy in copies[13:]:
        copy.wait()
    cot_send_ref[...] = close[6][1 - lax.axis_index("tower")]


def next_kernel(*refs):
    far, ins, close, refs = refs[:2], refs[2:8], refs[8:10], refs[10:]
    att_ref, *rest, sems = refs
    copies = begin(row_pairs(far[0], close[0], 4) + row_pairs(far[1], close[1], 4), sems)
    front_kernel(1, *ins[:5], *rest)
    attend(rest[-1], ins[5], att_ref)
    for copy in copies:
        copy.wait()


def fetch_kernel(*refs):
    count = len(refs) // 2
    for copy in begin(zip(refs[:count], refs[count : 2 * count]), refs[-1]):
        copy.wait()


def mid_kernel(
    seq,
    count_ref,
    rows_ref,
    att_ref,
    att_other_ref,
    norm_ref,
    wup_ref,
    wdown_ref,
    cot_ref,
    cot_other_ref,
    middle_ref,
    second_ref,
    final_ref,
    hidden_ref,
    pre_ref,
):
    length = rows_ref.shape[0]
    hidden_width = wup_ref.shape[1]
    attended = att_ref[...].astype(F32) + att_other_ref[...].astype(F32)
    middle = rows_ref[...].astype(F32) + attended
    middle_ref[...] = middle
    unit, _ = unit_and_scale(middle)
    norms = norm_ref[...].astype(F32)
    second = (unit * norms[2:3] + norms[3:4]).astype(BF)
    second_ref[...] = second
    valid = lax.broadcasted_iota(jnp.int32, (length, 1), 0) < count_ref[0:1, seq : seq + 1]
    cot = jnp.where(lax.axis_index("tower") == seq, cot_ref[seq], cot_other_ref[...])
    grad_final = jnp.where(valid, cot.astype(F32), 0.0).astype(BF)
    final_ref[...] = grad_final
    tile = 256
    for step in range(hidden_width // tile):
        cols = pl.ds(step * tile, tile)
        pre = dot(second, wup_ref[:, cols])
        grad_hidden = dot_t(grad_final, wdown_ref[cols, :])
        power = jnp.exp(pre * pre * -0.5)
        reach = 1.0 / (1.0 + jnp.abs(pre) * (0.3275911 / math.sqrt(2.0)))
        tail = (
            reach
            * (
                0.127414796
                + reach
                * (
                    -0.142248368
                    + reach * (0.7107068705 + reach * (-0.7265760135 + reach * 0.5307027145))
                )
            )
            * power
        )
        phi = jnp.where(pre >= 0.0, 1.0 - tail, tail)
        hidden_ref[:, cols] = (pre * phi).astype(BF)
        slope = phi + pre * (power * (1.0 / math.sqrt(2.0 * math.pi)))
        pre_ref[:, cols] = (grad_hidden * slope).astype(BF)


def sides_kernel(wup_ref, wdown_ref, hidden_ref, pre_ref, back_ref, out_ref):
    back_ref[...] = dot_t(pre_ref[...], wup_ref[...]).astype(BF)
    out_ref[...] = dot(hidden_ref[...], wdown_ref[...]).astype(BF)


def whole_mid_kernel(seq, *refs):
    mid_kernel(seq, *refs[:9], *refs[11:])
    sides_kernel(refs[5], refs[6], *refs[14:16], *refs[9:11])


def block_home(own, block, order):
    which = 1 - ((block >> order[0]) & 1) if own else (block >> order[0]) & 1
    return which, 2 * ((block >> order[1]) & 1) + ((block >> order[2]) & 1)


def store_blocks(order, stride, left, refs):
    rows = left.shape[0] // SPLIT
    own = (lax.axis_index("dp") // (stride << order[0])) & 1
    for side in range(2):

        @pl.when(own == side)
        def _():
            for block in range(SPLIT):
                which, place = block_home(side, block, order)
                refs[which][place * rows : (place + 1) * rows, :] = left[
                    block * rows : (block + 1) * rows
                ]


def halves_dot(left_ref, rights, cols):
    tokens = rights[0].shape[0]
    total = dot(left_ref[:, :tokens], rights[0][:, cols])
    return total + dot(left_ref[:, tokens:], rights[1][:, cols])


def send_kernel(order, stride, cols, lefts, rights, send_ref, keep_left_ref, send_left_ref):
    left = jnp.concatenate([r[...].T for r in lefts], axis=1)
    store_blocks(order, stride, left, (keep_left_ref, send_left_ref))
    send_ref[...] = halves_dot(send_left_ref, rights, cols).astype(BF).reshape(send_ref.shape)


def keep_kernel(cols, left_ref, rights, keep_ref):
    keep_ref[...] = halves_dot(left_ref, rights, cols).astype(BF).reshape(keep_ref.shape)


def copy_kernel(sources, target_ref):
    for place, source in enumerate(sources):
        target_ref[place] = source[...]


def mixer_a_kernel(
    order,
    stride,
    first_refs,
    mixed_refs,
    norm_own_ref,
    norm_other_ref,
    keep_ref,
    send_ref,
    first_scr,
):
    inner = mixed_refs[0].shape[2]
    store_blocks(
        order,
        stride,
        jnp.concatenate([r[...].T for r in first_refs], axis=1),
        (first_scr.at[0], first_scr.at[1]),
    )
    rows = first_scr.shape[1] // 4
    shape = (2, 2, rows, inner)
    mixed = [jnp.concatenate([r[part] for r in mixed_refs], axis=0) for part in range(2)]
    for which, ref in ((1, send_ref), (0, keep_ref)):
        for part in range(2):
            cols = slice(part * inner, (part + 1) * inner)
            ref[:, :, 0:rows, cols] = dot(first_scr[which], mixed[part]).astype(BF).reshape(shape)
        ref[:, :, rows:, :] = jnp.zeros((2, 2, 8, 2 * inner), BF)
    own_norm = norm_own_ref[...]
    row = lax.broadcasted_iota(jnp.int32, (8, 1), 0)
    norm_grad = own_norm + jnp.where(row < 2, norm_other_ref[...], 0.0)
    own = own_bit(order, 0, stride)
    for block in range(SPLIT):
        piece = norm_grad[:, block * rows : (block + 1) * rows].astype(BF)
        bits = [(block >> o) & 1 for o in order]

        @pl.when(own == bits[0])
        def _():
            keep_ref[bits[1], bits[2], rows:, 0:rows] = piece

        @pl.when(own != bits[0])
        def _():
            send_ref[bits[1], bits[2], rows:, 0:rows] = piece


def mixer_b_kernel(
    order,
    stride,
    mid_refs,
    ctx_refs,
    first_refs,
    mixed_refs,
    keep_ref,
    send_ref,
    first_scr,
    mid_scr,
):
    inner = ctx_refs[0].shape[1]
    store_blocks(
        order,
        stride,
        jnp.concatenate([r[...].T for r in first_refs], axis=1),
        (first_scr.at[0], first_scr.at[1]),
    )
    store_blocks(
        order,
        stride,
        jnp.concatenate([r[...].T for r in mid_refs], axis=1),
        (mid_scr.at[0], mid_scr.at[1]),
    )
    right = jnp.concatenate([r[...] for r in ctx_refs], axis=0)
    mixed = jnp.concatenate([r[2] for r in mixed_refs], axis=0)
    shape = keep_ref.shape[:3] + (inner,)
    for which, ref in ((1, send_ref), (0, keep_ref)):
        ref[:, :, :, 0:inner] = dot(first_scr[which], mixed).astype(BF).reshape(shape)
        ref[:, :, :, inner : 2 * inner] = dot(mid_scr[which], right).astype(BF).reshape(shape)


def back_kernel(
    own_ref,
    other_ref,
    middle_ref,
    final_ref,
    norm_ref,
    wout_ref,
    win_ref,
    qkv_ref,
    probs_ref,
    rows_ref,
    before_ref,
    first_ref,
    mid_ref,
    mixed_ref,
    norm_grad_ref,
    ctx_grad_scr,
):
    inner = wout_ref.shape[0]
    grad_second = own_ref[...].astype(F32) + other_ref[...].astype(F32)
    unit, scale = unit_and_scale(middle_ref[...])
    second_gain = jnp.sum(grad_second * unit, axis=0, keepdims=True)
    second_shift = jnp.sum(grad_second, axis=0, keepdims=True)
    gain = norm_ref[2:3].astype(F32)
    grad_mid = final_ref[...].astype(F32) + norm_back(grad_second, unit, scale, gain)
    grad_mid = grad_mid.astype(BF)
    mid_ref[...] = grad_mid
    ctx_grad_scr[...] = dot_t(grad_mid, wout_ref[...]).astype(BF)
    masks = half_masks()
    pairs = [pl.ds(pair * PAIR, PAIR) for pair in range(inner // PAIR)]
    halves, grad_probs, slopes = [], [], []
    for cols in pairs:
        grad_ctx = ctx_grad_scr[:, cols]
        for half in range(2):
            halves.append(grad_ctx * masks[half])
            grad_probs.append(dot_t(halves[-1], qkv_ref[2, :, cols]))
    for pair, cols in enumerate(pairs):
        both = slice(2 * pair, 2 * pair + 2)
        probs = jnp.concatenate([probs_ref[2 * pair], probs_ref[2 * pair + 1]], axis=0)
        grad_v = t_dot(probs, jnp.concatenate(halves[both], axis=0))
        mixed_ref[2, :, cols] = grad_v.astype(BF)
    for head, grad_prob in enumerate(grad_probs):
        prob = probs_ref[head].astype(F32)
        along = jnp.sum(prob * grad_prob, axis=-1, keepdims=True)
        slopes.append((prob * (grad_prob - along)).astype(BF))
    for pair, cols in enumerate(pairs):
        both = slice(2 * pair, 2 * pair + 2)
        queries, keys = qkv_ref[0, :, cols], qkv_ref[1, :, cols]
        key_stack = jnp.concatenate([keys * masks[0], keys * masks[1]], axis=0)
        query_stack = jnp.concatenate([queries * masks[0], queries * masks[1]], axis=0)
        grad_q = dot(jnp.concatenate(slopes[both], axis=1), key_stack) * HD**-0.5
        grad_k = t_dot(jnp.concatenate(slopes[both], axis=0), query_stack) * HD**-0.5
        mixed_ref[0, :, cols] = grad_q.astype(BF)
        mixed_ref[1, :, cols] = grad_k.astype(BF)
    total = dot_t(mixed_ref[0], win_ref[0])
    for part in range(1, 3):
        total += dot_t(mixed_ref[part], win_ref[part])
    first_ref[...] = total.astype(BF)
    unit, _ = unit_and_scale(rows_ref[...].astype(F32))
    norm_grad = jnp.concatenate(
        [
            jnp.sum(total * unit, axis=0, keepdims=True),
            jnp.sum(total, axis=0, keepdims=True),
            second_gain,
            second_shift,
            jnp.zeros((4, total.shape[1]), F32),
        ],
        axis=0,
    )
    norm_grad_ref[...] = norm_grad if before_ref is None else norm_grad + before_ref[...]


def input_kernel(
    order_ref, count_ref, own_ref, other_ref, rows_refs, mid_refs, norm_ref, out_ref
):
    length = rows_refs[0].shape[0]
    gain = norm_ref[0:1].astype(F32)
    for seq in range(len(rows_refs)):
        grad_first = own_ref[seq].astype(F32) + other_ref[seq].astype(F32)
        unit, scale = unit_and_scale(rows_refs[seq][...].astype(F32))
        grad_rows = mid_refs[seq][...].astype(F32) + norm_back(grad_first, unit, scale, gain)
        table = place_table(order_ref, count_ref[0:1, seq : seq + 1], seq, length)
        out_ref[seq] = dot(table, grad_rows.astype(BF)).astype(BF)


def final_kernel(count_ref, middle_refs, own_ref, other_ref, keep_ref, send_ref):
    length = middle_refs[0].shape[0]
    row = lax.broadcasted_iota(jnp.int32, (length, 1), 0)
    tower = lax.axis_index("tower")
    for seq in range(2):
        output = own_ref[seq].astype(F32) + other_ref[seq].astype(F32)
        final = jnp.where(row < count_ref[0:1, seq : seq + 1], middle_refs[seq][...] + output, 0.0).astype(BF)

        @pl.when(tower == seq)
        def _():
            keep_ref[...] = final

        @pl.when(tower != seq)
        def _():
            send_ref[...] = final


def join_kernel(keep_ref, other_ref, out_ref):
    tower = lax.axis_index("tower")
    out_ref[tower] = keep_ref[...]
    out_ref[1 - tower] = other_ref[...]


def update_values(gradient, master, moment, average, rate):
    moment_new = MOMENTUM * moment + gradient
    master_new = master - rate * (gradient + MOMENTUM * moment_new)
    average_new = AVERAGE_RATE * average + (1.0 - AVERAGE_RATE) * master_new
    return gradient, master_new, moment_new, average_new, master_new.astype(BF)


def update_kernel(rates, stride, groups, masters, moments, averages, *outs):
    total, norm_total = {}, None
    for place, chunks in enumerate(groups):
        rows = masters[place].shape[-2]
        pieces = []
        for order, parts in chunks:
            piece = gathered(order, stride, *parts) if len(parts) == 4 else parts[0][...]
            if len(parts) == 2:
                norm_total = parts[1][...]
            if piece.shape[0] > rows:
                norm_total = piece[rows : rows + 4, 0:rows]
            pieces.append(piece[0:rows])
        total[place] = jnp.concatenate(pieces, axis=1)
    first, start = total[0], 0
    for place, rate in enumerate(rates):
        group = outs[5 * place : 5 * place + 5]
        deep = masters[place].ndim == 3
        columns = masters[place].shape[-1]
        for piece in range(masters[place].shape[0] if deep else 1):
            at = piece if deep else Ellipsis
            if place == 2:
                gradient = norm_total
            elif place < len(groups):
                gradient = total[place][:, piece * columns : (piece + 1) * columns]
            else:
                gradient = first[:, start : start + columns]
            if place == 0:
                start += columns
            values = update_values(
                gradient, masters[place][at], moments[place][at], averages[place][at], rate
            )
            for ref, value in zip(group, values):
                ref[at] = value


def near(values):
    return pltpu.with_memory_space_constraint(values, pltpu.VMEM)


class Line:
    def __init__(self):
        self.token = None
        self.weight = 0

    def call(self, kernel, outs, *args, far=0, raw=0, scratch=()):
        flat, tree = jax.tree.flatten(args)
        flat = [pltpu.with_memory_space_constraint(v, pltpu.HBM) for v in flat[:raw]] + flat[raw:]
        extra = [] if self.token is None else [self.token]
        near_outs = [pltpu.VMEM(s, d) for s, d in outs[far:]]
        far_outs = [jax.ShapeDtypeStruct(s, d) for s, d in outs[:far]]
        count, gap = len(flat), len(extra)

        def body(*refs):
            ins = jax.tree.unflatten(tree, refs[:count])
            rest = refs[count + gap :]
            kernel(*ins, *rest[: len(outs)], *rest[len(outs) + 1 :])
            rest[len(outs)][...] = jnp.zeros((8, 128), F32)

        whole = pl.BlockSpec(memory_space=pltpu.VMEM)
        *results, self.token = pl.pallas_call(
            body,
            out_shape=far_outs + near_outs + [pltpu.VMEM((8, 128), F32)],
            in_specs=[pl.BlockSpec(memory_space=pltpu.HBM)] * raw + [whole] * (count + gap - raw),
            out_specs=[whole] * (len(outs) + 1),
            scratch_shapes=list(scratch),
            compiler_params=pltpu.CompilerParams(vmem_limit_bytes=VMEM_BYTES),
            cost_estimate=pl.CostEstimate(
                flops=int(self.weight * MICROSECOND), transcendentals=0, bytes_accessed=0
            ),
        )(*flat, *extra)
        return results


def swap(values, axis):
    return near(lax.ppermute(values, axis, [(0, 1), (1, 0)]))


def hop(values, bit, stride):
    size = lax.axis_size("dp")
    step = stride << bit
    return near(lax.ppermute(values, "dp", [(i, i ^ step) for i in range(size)]))


def own_bit(order, stage, stride):
    return (lax.axis_index("dp") // (stride << order[stage])) & 1


def second_kernel(order, stride, keep_ref, one_ref, send_ref):
    other = 1 - own_bit(order, 1, stride)
    total = keep_ref[other].astype(F32) + one_ref[other].astype(F32)
    send_ref[...] = total.astype(send_ref.dtype)


def third_kernel(order, stride, keep_ref, one_ref, two_ref, send_ref):
    own = own_bit(order, 1, stride)
    other = 1 - own_bit(order, 2, stride)
    total = keep_ref[own, other].astype(F32) + one_ref[own, other].astype(F32)
    send_ref[...] = (total + two_ref[other].astype(F32)).astype(send_ref.dtype)


def gathered(order, stride, keep_ref, one_ref, two_ref, three_ref):
    two, three = own_bit(order, 1, stride), own_bit(order, 2, stride)
    total = keep_ref[two, three].astype(F32) + one_ref[two, three].astype(F32)
    return total + two_ref[three].astype(F32) + three_ref[...].astype(F32)


class Chunk:
    def __init__(self, line, keep, send, order, stride):
        self.line, self.order, self.stride = line, order, stride
        self.parts = [keep, hop(send, order[0], stride)]

    def step(self):
        keep = self.parts[0]
        stage = len(self.parts) - 1
        kernel = (second_kernel, third_kernel)[stage - 1]
        (send,) = self.line.call(
            functools.partial(kernel, self.order, self.stride),
            [(keep.shape[stage:], keep.dtype)],
            *self.parts,
        )
        self.parts.append(hop(send, self.order[stage], self.stride))


def total_kernel(order, stride, parts, total_ref):
    total_ref[...] = gathered(order, stride, *parts)


def scatter_rest(line, chunk, rows):
    (total,) = line.call(
        functools.partial(total_kernel, chunk.order, chunk.stride),
        [(chunk.parts[3].shape, F32)],
        chunk.parts,
        far=1,
    )
    size, stride = lax.axis_size("dp"), chunk.stride
    groups = [[g * stride + i for i in range(stride)] for g in range(size // stride)]

    def scatter(values, dimension):
        return near(
            lax.psum_scatter(
                values, "dp", scatter_dimension=dimension, axis_index_groups=groups, tiled=True
            )
        )

    if total.shape[0] == rows:
        return [scatter(total, 0)]
    return [scatter(total[:rows], 0), scatter(total[rows : rows + 4, :rows], 1)]


def shards(
    tower_input,
    patch_order,
    visible_count,
    joint_cotangent,
    mixer_in_copy,
    mixer_in_master,
    mixer_in_moment,
    mixer_in_average,
    mixer_out_copy,
    mixer_out_master,
    mixer_out_moment,
    mixer_out_average,
    expand_copy,
    expand_master,
    expand_moment,
    expand_average,
    contract_copy,
    contract_master,
    contract_moment,
    contract_average,
    norm_params_copy,
    norm_params_master,
    norm_params_moment,
    norm_params_average,
):
    seq_count, length, width = tower_input.shape[1:]
    inner = mixer_in_copy.shape[3]
    heads = inner // HD
    hidden_width = expand_copy.shape[2]
    dp_size = lax.axis_size("dp")
    stride = dp_size // SPLIT
    tower = lax.axis_index("tower")
    line = Line()
    act = (length, width)
    both = ((seq_count,) + act, BF)
    tokens = seq_count * length
    left_scratch = pltpu.VMEM((2, width // 2, tokens), BF)
    front_outs = [
        (act, BF),
        (act, BF),
        ((3, length, inner), BF),
        ((heads, length, length), BF),
        ((length, inner), BF),
    ]
    got, chunks = {}, {}

    def lead():
        far = [
            patch_order,
            visible_count,
            tower_input[0],
            jnp.transpose(mixer_in_copy[0], (1, 0, 2)),
            norm_params_copy[0],
            mixer_out_copy[0],
            joint_cotangent.reshape(2, length, width),
        ]
        results = line.call(
            lead_kernel,
            [(v.shape, v.dtype) for v in far] + [(act, BF), (act, BF)] + front_outs,
            *far,
            raw=len(far),
            scratch=[pltpu.SemaphoreType.DMA((16,))],
        )
        got["fixed"], got["att0"], got["front0"] = results[:7], results[7], results[9:]
        got["cot_other"] = swap(results[8], "tower")
        got["att0_other"] = swap(results[7], "mp")

    def following():
        far = [expand_copy[0], contract_copy[0]]
        w_up, w_down, att, *front = line.call(
            next_kernel,
            [(v.shape, v.dtype) for v in far] + [(act, BF)] + front_outs,
            *far,
            *got["fixed"][:6],
            raw=len(far),
            scratch=[pltpu.SemaphoreType.DMA((8,))],
        )
        got["wide"], got["att1"], got["front1"] = (w_up, w_down), att, front
        got["att1_other"] = swap(att, "mp")

    mid_outs = [
        (act, F32),
        (act, BF),
        (act, BF),
        ((length, hidden_width), BF),
        ((length, hidden_width), BF),
    ]

    def mid(seq):
        _, count, _, _, norms, _, cot = got["fixed"]
        kernel, outs = (mid_kernel, []) if seq else (whole_mid_kernel, [(act, BF)] * 2)
        results = line.call(
            functools.partial(kernel, seq),
            outs + mid_outs,
            count,
            got[f"front{seq}"][0],
            got[f"att{seq}"],
            got[f"att{seq}_other"],
            norms,
            *got["wide"],
            cot,
            got["cot_other"],
        )
        if seq:
            got["mid1"] = [None, None] + results
        else:
            got["mid0"] = results
            got["back_other0"] = swap(results[0], "mp")

    def sides():
        hidden, pre = got["mid1"][5:7]
        results = line.call(sides_kernel, [(act, BF)] * 2, *got["wide"], hidden, pre)
        got["mid1"][0:2] = results
        got["back_other1"] = swap(results[0], "mp")

    def pick(name, place):
        return [got[f"{name}{seq}"][place] for seq in range(2)]

    def group(index):
        source, start, stop, order = GROUPS[index]
        cols = slice(start * hidden_width // 6, stop * hidden_width // 6)
        shape = ((2, 2, width // SPLIT, cols.stop - cols.start), BF)
        lefts, rights = ((4, 5), (3, 6))[source]
        send, left = line.call(
            functools.partial(send_kernel, order, stride, cols),
            [shape, ((width // 2, tokens), BF)],
            pick("mid", lefts),
            pick("mid", rights),
            scratch=[pltpu.VMEM((width // 2, tokens), BF)],
        )
        chunks[f"C{index}"] = Chunk(line, None, send, order, stride)
        got[f"rest{index}"] = (cols, shape, left, pick("mid", rights))

    def rest(index):
        cols, shape, left, rights = got[f"rest{index}"]
        (chunks[f"C{index}"].parts[0],) = line.call(
            functools.partial(keep_kernel, cols), [shape], left, rights
        )

    def back(seq):
        _, _, _, w_in, norms, w_out, _ = got["fixed"]
        rows, _, qkv, probs, _ = got[f"front{seq}"]
        first, _, middle, _, final, _, _ = got[f"mid{seq}"]
        got[f"last{seq}"] = line.call(
            back_kernel,
            [(act, BF), (act, BF), ((3, length, inner), BF), ((8, width), F32)],
            first,
            got[f"back_other{seq}"],
            middle,
            final,
            norms,
            w_out,
            w_in,
            qkv,
            probs,
            rows,
            got["last0"][3] if seq else None,
            scratch=[pltpu.VMEM((length, inner), BF)],
        )
        if seq:
            got["norm_other"] = swap(got["last1"][3], "mp")

    def share(name, sources):
        (result,) = line.call(copy_kernel, [both], sources)
        got[name], got[name + "_other"] = result, swap(result, "mp")

    def mixer_a():
        keep, send = line.call(
            functools.partial(mixer_a_kernel, A_ORDER, stride),
            [((2, 2, width // SPLIT + 8, 2 * inner), BF)] * 2,
            pick("front", 1),
            pick("last", 2),
            got["last1"][3],
            got["norm_other"],
            scratch=[left_scratch],
        )
        chunks["M0"] = Chunk(line, keep, send, A_ORDER, stride)

    def mixer_b():
        keep, send = line.call(
            functools.partial(mixer_b_kernel, MIX_ORDER, stride),
            [((2, 2, width // SPLIT, 2 * inner), BF)] * 2,
            pick("last", 1),
            pick("front", 4),
            pick("front", 1),
            pick("last", 2),
            scratch=[left_scratch] * 2,
        )
        chunks["M1"] = Chunk(line, keep, send, MIX_ORDER, stride)

    def fetch_masters():
        far = [
            *[jnp.transpose(v[0], (1, 0, 2)) for v in (mixer_in_master, mixer_in_moment, mixer_in_average)],
            *[v[0].T for v in (mixer_out_master, mixer_out_moment, mixer_out_average)],
            *[v[0] for v in (norm_params_master, norm_params_moment, norm_params_average)],
            *[v[0].T for v in (contract_master, contract_moment, contract_average)],
            *[v[0] for v in (expand_master, expand_moment, expand_average)],
        ]
        got["masters"] = line.call(
            fetch_kernel,
            [(v.shape, v.dtype) for v in far],
            *far,
            raw=len(far),
            scratch=[pltpu.SemaphoreType.DMA((len(far),))],
        )

    def input_side():
        patches, count, _, _, norms, _, _ = got["fixed"]
        (got["input_grad"],) = line.call(
            input_kernel,
            [both],
            patches,
            count,
            got["firsts"],
            got["firsts_other"],
            pick("front", 0),
            pick("last", 1),
            norms,
            far=1,
        )

    def final_side():
        got["keep"], send = line.call(
            final_kernel,
            [(act, BF), (act, BF)],
            got["fixed"][1],
            pick("mid", 2),
            got["outs"],
            got["outs_other"],
        )
        got["row_other"] = swap(send, "tower")

    def join():
        (got["joint"],) = line.call(
            join_kernel, [((2, length, width), BF)], got["keep"], got["row_other"], far=1
        )

    rate_scale = 1.0 / math.sqrt(seq_count * dp_size * length)

    def update(name, names, start, indices):
        lists = [[chunks[n] for n in group_names] for group_names in names]
        weights = [got["masters"][3 * i : 3 * i + 3] for i in range(start, start + len(indices))]
        sizes = [g[0].shape for g in weights]
        groups = []
        for members in lists:
            groups.append(
                [
                    (c.order, scatter_rest(line, c, width // SPLIT) if stride > 1 else c.parts)
                    for c in members
                ]
            )
        orders = [[order for order, _ in members] for members in groups]

        def kernel(parts, *refs):
            paired = [list(zip(o, p)) for o, p in zip(orders, parts)]
            update_kernel([STEP_RATES[i] * rate_scale for i in indices], stride, paired, *refs)

        values = line.call(
            kernel,
            [(s, F32 if i < 4 else BF) for s in sizes for i in range(5)],
            [[parts for _, parts in members] for members in groups],
            *[[g[i] for g in weights] for i in range(3)],
            far=5 * len(weights),
        )
        got[name] = [values[5 * i : 5 * i + 5] for i in range(len(weights))]

    def source_names(source):
        return [f"C{i}" for i, g in enumerate(GROUPS) if g[0] == source]

    steps = {
        "lead": lead,
        "next": following,
        "mid0": lambda: mid(0),
        "mid1": lambda: mid(1),
        "sides": sides,
        "back0": lambda: back(0),
        "back1": lambda: back(1),
        "cpA4": lambda: share("firsts", pick("last", 0)),
        "cpA2": lambda: share("outs", pick("mid", 1)),
        "fetch": fetch_masters,
        "kM0": mixer_a,
        "kM1": mixer_b,
        "inp": input_side,
        "fin": final_side,
        "join": join,
        "updC": lambda: update("down", [source_names(0)], 3, (3,)),
        "updE": lambda: update("up", [source_names(1)], 4, (2,)),
        "updM": lambda: update("mixer", [["M0", "M1"]], 0, (0, 1, 4)),
    }
    for name, weight in PLAN:
        line.weight = weight
        if name in steps:
            steps[name]()
        elif name.startswith("kC"):
            group(int(name[2:]))
        elif name.startswith("hC"):
            rest(int(name[2:]))
        else:
            chunks[name[2:]].step()

    in_set, out_set, norm_set = got["mixer"]
    (down_set,), (up_set,) = got["down"], got["up"]
    return (
        got["joint"].reshape(1, 1, 2, seq_count // 2, length, width),
        got["input_grad"][None],
        *[jnp.transpose(v, (1, 0, 2))[None] for v in in_set],
        *[v.T[None] for v in out_set],
        *[v[None] for v in up_set],
        *[v.T[None] for v in down_set],
        *[v[None] for v in norm_set],
    )


def solution(mesh):
    weight_in = P("tower", "dp", None, "mp")
    weight_out = P("tower", "mp", "dp")
    weight_up = P("tower", "dp", "mp")
    norm = P("tower", None, "dp")
    return jax.shard_map(
        shards,
        mesh=mesh,
        in_specs=(
            P("tower", "dp", None, None),
            P("dp", None),
            P("tower", "dp"),
            P("dp", "tower", None, None, None, None),
            P("tower", None, None, "mp"),
            *[weight_in] * 3,
            P("tower", "mp", None),
            *[weight_out] * 3,
            P("tower", None, "mp"),
            *[weight_up] * 3,
            P("tower", "mp", None),
            *[weight_out] * 3,
            P("tower", None, None),
            *[norm] * 3,
        ),
        out_specs=(
            P("dp", "tower", None, None, None, None),
            P("tower", "dp", None, None),
            *[weight_in] * 5,
            *[weight_out] * 5,
            *[weight_up] * 5,
            *[weight_out] * 5,
            *[norm] * 5,
        ),
        check_vma=False,
    )
```

```python
import functools
import math

import jax
import jax.numpy as jnp
from jax import lax
from jax.experimental import pallas as pl
from jax.experimental.pallas import tpu as pltpu
from jax.sharding import PartitionSpec as P

HD = 64
PAIR = 2 * HD
EPSILON = 1e-06
MOMENTUM = 0.9
AVERAGE_RATE = 0.6
STEP_RATES = (0.013, 1.3, 0.06, 0.015, 0.04)
SPLIT = 8
MICROSECOND = 1153500000
A_ORDER, B_ORDER = (0, 1, 2), (1, 0, 2)
MIX_ORDER = A_ORDER
GROUPS = ((0, 0, 6, A_ORDER), (1, 0, 6, B_ORDER))
PLAN = (
    ("lead", 6),
    ("next", 20),
    ("mid0", 3),
    ("mid1", 8),
    ("kC0", 2),
    ("sides", 0.5),
    ("kC1", 1),
    ("back0", 1),
    ("back1", 1),
    ("hC0", 0.5),
    ("kM0", 4),
    ("hC1", 1),
    ("s2C0", 4),
    ("s2C1", 40),
    ("cpA2", 4),
    ("kM1", 0.5),
    ("s3C0", 8),
    ("s2M0", 12),
    ("fetch", 0.5),
    ("fin", 2),
    ("s3C1", 0),
    ("cpA4", 1),
    ("updC", 8),
    ("s2M1", 20),
    ("s3M0", 1),
    ("updE", 3),
    ("join", 4),
    ("s3M1", 6),
    ("inp", 0),
    ("updM", 0),
)
BF = jnp.bfloat16
F32 = jnp.float32
VMEM_BYTES = 8 * 1024 * 1024


def dot(left, right):
    return lax.dot_general(left, right, (((1,), (0,)), ((), ())), preferred_element_type=F32)


def dot_t(left, right):
    return lax.dot_general(left, right, (((1,), (1,)), ((), ())), preferred_element_type=F32)


def t_dot(left, right):
    return lax.dot_general(left, right, (((0,), (0,)), ((), ())), preferred_element_type=F32)


def unit_and_scale(rows):
    centred = rows - jnp.mean(rows, axis=-1, keepdims=True)
    spread = jnp.mean(centred * centred, axis=-1, keepdims=True)
    scale = lax.rsqrt(spread + EPSILON)
    return centred * scale, scale


def norm_back(grad_out, unit, scale, gain):
    grad_unit = grad_out * gain
    inner = jnp.mean(grad_unit, axis=-1, keepdims=True)
    along = jnp.mean(grad_unit * unit, axis=-1, keepdims=True)
    return scale * (grad_unit - inner - unit * along)


def half_masks():
    lane = lax.broadcasted_iota(jnp.int32, (1, PAIR), 1)
    return [jnp.where(lane < HD, 1.0, 0.0).astype(BF), jnp.where(lane < HD, 0.0, 1.0).astype(BF)]


def place_table(order_ref, count, seq, length):
    slot = lax.broadcasted_iota(jnp.int32, (length, length), 0)
    lane = lax.broadcasted_iota(jnp.int32, (length, length), 1)
    own = jnp.where(lax.axis_index("tower") == 0, order_ref[seq : seq + 1, :], lane[0:1, :])
    return jnp.where((slot == own) & (lane < count), 1.0, 0.0).astype(BF)


def front_kernel(
    seq,
    order_ref,
    count_ref,
    x_ref,
    win_ref,
    norm_ref,
    rows_ref,
    first_ref,
    qkv_ref,
    probs_ref,
    ctx_ref,
    waits=(),
):
    length = x_ref.shape[1]
    inner = win_ref.shape[2]
    hold(waits, 0)
    count = count_ref[0:1, seq : seq + 1]
    table = place_table(order_ref, count, seq, length)
    rows = t_dot(table, x_ref[seq])
    rows_ref[...] = rows.astype(BF)
    unit, _ = unit_and_scale(rows)
    norms = norm_ref[...].astype(F32)
    first = (unit * norms[0:1] + norms[1:2]).astype(BF)
    first_ref[...] = first
    for part in range(3):
        hold(waits, 1 + part)
        qkv_ref[part] = dot(first, win_ref[part]).astype(BF)
    masks = half_masks()
    key_lane = lax.broadcasted_iota(jnp.int32, (1, length), 1) < count
    pairs = [pl.ds(pair * PAIR, PAIR) for pair in range(inner // PAIR)]
    scores = []
    for cols in pairs:
        for half in range(2):
            queries = qkv_ref[0, :, cols] * (masks[half] * HD**-0.5).astype(BF)
            scores.append(jnp.where(key_lane, dot_t(queries, qkv_ref[1, :, cols]), -1e30))
    probs = []
    for head, score in enumerate(scores):
        powers = jnp.exp(score - jnp.max(score, axis=-1, keepdims=True))
        low = (powers * (1.0 / jnp.sum(powers, axis=-1, keepdims=True))).astype(BF)
        probs_ref[head] = low
        probs.append(low)
    for pair, cols in enumerate(pairs):
        values = qkv_ref[2, :, cols]
        stacked = jnp.concatenate([values * masks[0], values * masks[1]], axis=0)
        both = jnp.concatenate(probs[2 * pair : 2 * pair + 2], axis=1)
        ctx_ref[:, cols] = dot(both, stacked).astype(BF)


def hold(waits, place):
    for copy in waits[place] if waits else ():
        copy.wait()


def begin(pairs, sems):
    copies = [
        pltpu.make_async_copy(source, target, sems.at[i])
        for i, (source, target) in enumerate(pairs)
    ]
    for copy in copies:
        copy.start()
    return copies


def row_pairs(source, target, parts):
    rows = source.shape[0] // parts
    cuts = [pl.ds(i * rows, rows) for i in range(parts)]
    return [(source.at[cut], target.at[cut]) for cut in cuts]


def attend(ctx_ref, wout_ref, att_ref):
    att_ref[...] = dot(ctx_ref[...], wout_ref[...]).astype(BF)


def lead_kernel(*refs):
    far, close, refs = refs[:7], refs[7:14], refs[14:]
    att_ref, cot_send_ref, *rest, sems = refs
    pairs = [(far[i], close[i]) for i in (0, 1, 4)]
    pairs.append((far[2].at[0], close[2].at[0]))
    for part in range(3):
        pairs.append((far[3].at[part], close[3].at[part]))
    pairs.append((far[5], close[5]))
    for seq in range(2):
        pairs += row_pairs(far[6].at[seq], close[6].at[seq], 1)
    pairs += row_pairs(far[2].at[1], close[2].at[1], 1)
    copies = begin(pairs, sems)
    waits = [copies[0:4], copies[4:5], copies[5:6], copies[6:7]]
    front_kernel(0, *close[:5], *rest, waits=waits)
    for copy in copies[7:8]:
        copy.wait()
    attend(rest[-1], close[5], att_ref)
    for copy in copies[8:]:
        copy.wait()
    cot_send_ref[...] = close[6][1 - lax.axis_index("tower")]


def next_kernel(*refs):
    far, ins, close, refs = refs[:2], refs[2:8], refs[8:10], refs[10:]
    att_ref, *rest, sems = refs
    copies = begin(row_pairs(far[0], close[0], 4) + row_pairs(far[1], close[1], 4), sems)
    front_kernel(1, *ins[:5], *rest)
    attend(rest[-1], ins[5], att_ref)
    for copy in copies:
        copy.wait()


def fetch_kernel(*refs):
    count = len(refs) // 2
    for copy in begin(zip(refs[:count], refs[count : 2 * count]), refs[-1]):
        copy.wait()


def mid_kernel(
    seq,
    count_ref,
    rows_ref,
    att_ref,
    att_other_ref,
    norm_ref,
    wup_ref,
    wdown_ref,
    cot_ref,
    cot_other_ref,
    middle_ref,
    second_ref,
    final_ref,
    hidden_ref,
    pre_ref,
):
    length = rows_ref.shape[0]
    hidden_width = wup_ref.shape[1]
    attended = att_ref[...].astype(F32) + att_other_ref[...].astype(F32)
    middle = rows_ref[...].astype(F32) + attended
    middle_ref[...] = middle
    unit, _ = unit_and_scale(middle)
    norms = norm_ref[...].astype(F32)
    second = (unit * norms[2:3] + norms[3:4]).astype(BF)
    second_ref[...] = second
    valid = lax.broadcasted_iota(jnp.int32, (length, 1), 0) < count_ref[0:1, seq : seq + 1]
    cot = jnp.where(lax.axis_index("tower") == seq, cot_ref[seq], cot_other_ref[...])
    grad_final = jnp.where(valid, cot.astype(F32), 0.0).astype(BF)
    final_ref[...] = grad_final
    tile = 256
    for step in range(hidden_width // tile):
        cols = pl.ds(step * tile, tile)
        pre = dot(second, wup_ref[:, cols])
        grad_hidden = dot_t(grad_final, wdown_ref[cols, :])
        power = jnp.exp(pre * pre * -0.5)
        reach = 1.0 / (1.0 + jnp.abs(pre) * (0.3275911 / math.sqrt(2.0)))
        tail = (
            reach
            * (
                0.127414796
                + reach
                * (
                    -0.142248368
                    + reach * (0.7107068705 + reach * (-0.7265760135 + reach * 0.5307027145))
                )
            )
            * power
        )
        phi = jnp.where(pre >= 0.0, 1.0 - tail, tail)
        hidden_ref[:, cols] = (pre * phi).astype(BF)
        slope = phi + pre * (power * (1.0 / math.sqrt(2.0 * math.pi)))
        pre_ref[:, cols] = (grad_hidden * slope).astype(BF)


def sides_kernel(wup_ref, wdown_ref, hidden_ref, pre_ref, back_ref, out_ref):
    back_ref[...] = dot_t(pre_ref[...], wup_ref[...]).astype(BF)
    out_ref[...] = dot(hidden_ref[...], wdown_ref[...]).astype(BF)


def whole_mid_kernel(seq, *refs):
    mid_kernel(seq, *refs[:9], *refs[11:])
    sides_kernel(refs[5], refs[6], *refs[14:16], *refs[9:11])


def block_home(own, block, order):
    which = 1 - ((block >> order[0]) & 1) if own else (block >> order[0]) & 1
    return which, 2 * ((block >> order[1]) & 1) + ((block >> order[2]) & 1)


def store_blocks(order, stride, left, refs):
    rows = left.shape[0] // SPLIT
    own = (lax.axis_index("dp") // (stride << order[0])) & 1
    for side in range(2):

        @pl.when(own == side)
        def _():
            for block in range(SPLIT):
                which, place = block_home(side, block, order)
                refs[which][place * rows : (place + 1) * rows, :] = left[
                    block * rows : (block + 1) * rows
                ]


def halves_dot(left_ref, rights, cols):
    tokens = rights[0].shape[0]
    total = dot(left_ref[:, :tokens], rights[0][:, cols])
    return total + dot(left_ref[:, tokens:], rights[1][:, cols])


def send_kernel(order, stride, cols, lefts, rights, send_ref, keep_left_ref, send_left_ref):
    left = jnp.concatenate([r[...].T for r in lefts], axis=1)
    store_blocks(order, stride, left, (keep_left_ref, send_left_ref))
    send_ref[...] = halves_dot(send_left_ref, rights, cols).astype(BF).reshape(send_ref.shape)


def keep_kernel(cols, left_ref, rights, keep_ref):
    keep_ref[...] = halves_dot(left_ref, rights, cols).astype(BF).reshape(keep_ref.shape)


def copy_kernel(sources, target_ref):
    for place, source in enumerate(sources):
        target_ref[place] = source[...]


def mixer_a_kernel(
    order,
    stride,
    first_refs,
    mixed_refs,
    norm_own_ref,
    norm_other_ref,
    keep_ref,
    send_ref,
    first_scr,
):
    inner = mixed_refs[0].shape[2]
    store_blocks(
        order,
        stride,
        jnp.concatenate([r[...].T for r in first_refs], axis=1),
        (first_scr.at[0], first_scr.at[1]),
    )
    rows = first_scr.shape[1] // 4
    shape = (2, 2, rows, inner)
    mixed = [jnp.concatenate([r[part] for r in mixed_refs], axis=0) for part in range(2)]
    for which, ref in ((1, send_ref), (0, keep_ref)):
        for part in range(2):
            cols = slice(part * inner, (part + 1) * inner)
            ref[:, :, 0:rows, cols] = dot(first_scr[which], mixed[part]).astype(BF).reshape(shape)
        ref[:, :, rows:, :] = jnp.zeros((2, 2, 8, 2 * inner), BF)
    own_norm = norm_own_ref[...]
    row = lax.broadcasted_iota(jnp.int32, (8, 1), 0)
    norm_grad = own_norm + jnp.where(row < 2, norm_other_ref[...], 0.0)
    own = own_bit(order, 0, stride)
    for block in range(SPLIT):
        piece = norm_grad[:, block * rows : (block + 1) * rows].astype(BF)
        bits = [(block >> o) & 1 for o in order]

        @pl.when(own == bits[0])
        def _():
            keep_ref[bits[1], bits[2], rows:, 0:rows] = piece

        @pl.when(own != bits[0])
        def _():
            send_ref[bits[1], bits[2], rows:, 0:rows] = piece


def mixer_b_kernel(
    order,
    stride,
    mid_refs,
    ctx_refs,
    first_refs,
    mixed_refs,
    keep_ref,
    send_ref,
    first_scr,
    mid_scr,
):
    inner = ctx_refs[0].shape[1]
    store_blocks(
        order,
        stride,
        jnp.concatenate([r[...].T for r in first_refs], axis=1),
        (first_scr.at[0], first_scr.at[1]),
    )
    store_blocks(
        order,
        stride,
        jnp.concatenate([r[...].T for r in mid_refs], axis=1),
        (mid_scr.at[0], mid_scr.at[1]),
    )
    right = jnp.concatenate([r[...] for r in ctx_refs], axis=0)
    mixed = jnp.concatenate([r[2] for r in mixed_refs], axis=0)
    shape = keep_ref.shape[:3] + (inner,)
    for which, ref in ((1, send_ref), (0, keep_ref)):
        ref[:, :, :, 0:inner] = dot(first_scr[which], mixed).astype(BF).reshape(shape)
        ref[:, :, :, inner : 2 * inner] = dot(mid_scr[which], right).astype(BF).reshape(shape)


def back_kernel(
    own_ref,
    other_ref,
    middle_ref,
    final_ref,
    norm_ref,
    wout_ref,
    win_ref,
    qkv_ref,
    probs_ref,
    rows_ref,
    before_ref,
    first_ref,
    mid_ref,
    mixed_ref,
    norm_grad_ref,
    ctx_grad_scr,
):
    inner = wout_ref.shape[0]
    grad_second = own_ref[...].astype(F32) + other_ref[...].astype(F32)
    unit, scale = unit_and_scale(middle_ref[...])
    second_gain = jnp.sum(grad_second * unit, axis=0, keepdims=True)
    second_shift = jnp.sum(grad_second, axis=0, keepdims=True)
    gain = norm_ref[2:3].astype(F32)
    grad_mid = final_ref[...].astype(F32) + norm_back(grad_second, unit, scale, gain)
    grad_mid = grad_mid.astype(BF)
    mid_ref[...] = grad_mid
    ctx_grad_scr[...] = dot_t(grad_mid, wout_ref[...]).astype(BF)
    masks = half_masks()
    pairs = [pl.ds(pair * PAIR, PAIR) for pair in range(inner // PAIR)]
    halves, grad_probs, slopes = [], [], []
    for cols in pairs:
        grad_ctx = ctx_grad_scr[:, cols]
        for half in range(2):
            halves.append(grad_ctx * masks[half])
            grad_probs.append(dot_t(halves[-1], qkv_ref[2, :, cols]))
    for pair, cols in enumerate(pairs):
        both = slice(2 * pair, 2 * pair + 2)
        probs = jnp.concatenate([probs_ref[2 * pair], probs_ref[2 * pair + 1]], axis=0)
        grad_v = t_dot(probs, jnp.concatenate(halves[both], axis=0))
        mixed_ref[2, :, cols] = grad_v.astype(BF)
    for head, grad_prob in enumerate(grad_probs):
        prob = probs_ref[head].astype(F32)
        along = jnp.sum(prob * grad_prob, axis=-1, keepdims=True)
        slopes.append((prob * (grad_prob - along)).astype(BF))
    for pair, cols in enumerate(pairs):
        both = slice(2 * pair, 2 * pair + 2)
        queries, keys = qkv_ref[0, :, cols], qkv_ref[1, :, cols]
        key_stack = jnp.concatenate([keys * masks[0], keys * masks[1]], axis=0)
        query_stack = jnp.concatenate([queries * masks[0], queries * masks[1]], axis=0)
        grad_q = dot(jnp.concatenate(slopes[both], axis=1), key_stack) * HD**-0.5
        grad_k = t_dot(jnp.concatenate(slopes[both], axis=0), query_stack) * HD**-0.5
        mixed_ref[0, :, cols] = grad_q.astype(BF)
        mixed_ref[1, :, cols] = grad_k.astype(BF)
    total = dot_t(mixed_ref[0], win_ref[0])
    for part in range(1, 3):
        total += dot_t(mixed_ref[part], win_ref[part])
    first_ref[...] = total.astype(BF)
    unit, _ = unit_and_scale(rows_ref[...].astype(F32))
    norm_grad = jnp.concatenate(
        [
            jnp.sum(total * unit, axis=0, keepdims=True),
            jnp.sum(total, axis=0, keepdims=True),
            second_gain,
            second_shift,
            jnp.zeros((4, total.shape[1]), F32),
        ],
        axis=0,
    )
    norm_grad_ref[...] = norm_grad if before_ref is None else norm_grad + before_ref[...]


def input_kernel(
    order_ref, count_ref, own_ref, other_ref, rows_refs, mid_refs, norm_ref, out_ref
):
    length = rows_refs[0].shape[0]
    gain = norm_ref[0:1].astype(F32)
    for seq in range(len(rows_refs)):
        grad_first = own_ref[seq].astype(F32) + other_ref[seq].astype(F32)
        unit, scale = unit_and_scale(rows_refs[seq][...].astype(F32))
        grad_rows = mid_refs[seq][...].astype(F32) + norm_back(grad_first, unit, scale, gain)
        table = place_table(order_ref, count_ref[0:1, seq : seq + 1], seq, length)
        out_ref[seq] = dot(table, grad_rows.astype(BF)).astype(BF)


def final_kernel(count_ref, middle_refs, own_ref, other_ref, keep_ref, send_ref):
    length = middle_refs[0].shape[0]
    row = lax.broadcasted_iota(jnp.int32, (length, 1), 0)
    tower = lax.axis_index("tower")
    for seq in range(2):
        output = own_ref[seq].astype(F32) + other_ref[seq].astype(F32)
        final = jnp.where(row < count_ref[0:1, seq : seq + 1], middle_refs[seq][...] + output, 0.0).astype(BF)

        @pl.when(tower == seq)
        def _():
            keep_ref[...] = final

        @pl.when(tower != seq)
        def _():
            send_ref[...] = final


def join_kernel(keep_ref, other_ref, out_ref):
    tower = lax.axis_index("tower")
    out_ref[tower] = keep_ref[...]
    out_ref[1 - tower] = other_ref[...]


def update_values(gradient, master, moment, average, rate):
    moment_new = MOMENTUM * moment + gradient
    master_new = master - rate * (gradient + MOMENTUM * moment_new)
    average_new = AVERAGE_RATE * average + (1.0 - AVERAGE_RATE) * master_new
    return gradient, master_new, moment_new, average_new, master_new.astype(BF)


def update_kernel(rates, stride, groups, masters, moments, averages, *outs):
    total, norm_total = {}, None
    for place, chunks in enumerate(groups):
        rows = masters[place].shape[-2]
        pieces = []
        for order, parts in chunks:
            piece = gathered(order, stride, *parts) if len(parts) == 4 else parts[0][...]
            if len(parts) == 2:
                norm_total = parts[1][...]
            if piece.shape[0] > rows:
                norm_total = piece[rows : rows + 4, 0:rows]
            pieces.append(piece[0:rows])
        total[place] = jnp.concatenate(pieces, axis=1)
    first, start = total[0], 0
    for place, rate in enumerate(rates):
        group = outs[5 * place : 5 * place + 5]
        deep = masters[place].ndim == 3
        columns = masters[place].shape[-1]
        for piece in range(masters[place].shape[0] if deep else 1):
            at = piece if deep else Ellipsis
            if place == 2:
                gradient = norm_total
            elif place < len(groups):
                gradient = total[place][:, piece * columns : (piece + 1) * columns]
            else:
                gradient = first[:, start : start + columns]
            if place == 0:
                start += columns
            values = update_values(
                gradient, masters[place][at], moments[place][at], averages[place][at], rate
            )
            for ref, value in zip(group, values):
                ref[at] = value


def near(values):
    return pltpu.with_memory_space_constraint(values, pltpu.VMEM)


class Line:
    def __init__(self):
        self.token = None
        self.weight = 0

    def call(self, kernel, outs, *args, far=0, raw=0, scratch=()):
        flat, tree = jax.tree.flatten(args)
        flat = [pltpu.with_memory_space_constraint(v, pltpu.HBM) for v in flat[:raw]] + flat[raw:]
        extra = [] if self.token is None else [self.token]
        near_outs = [pltpu.VMEM(s, d) for s, d in outs[far:]]
        far_outs = [jax.ShapeDtypeStruct(s, d) for s, d in outs[:far]]
        count, gap = len(flat), len(extra)

        def body(*refs):
            ins = jax.tree.unflatten(tree, refs[:count])
            rest = refs[count + gap :]
            kernel(*ins, *rest[: len(outs)], *rest[len(outs) + 1 :])
            rest[len(outs)][...] = jnp.zeros((8, 128), F32)

        whole = pl.BlockSpec(memory_space=pltpu.VMEM)
        *results, self.token = pl.pallas_call(
            body,
            out_shape=far_outs + near_outs + [pltpu.VMEM((8, 128), F32)],
            in_specs=[pl.BlockSpec(memory_space=pltpu.HBM)] * raw + [whole] * (count + gap - raw),
            out_specs=[whole] * (len(outs) + 1),
            scratch_shapes=list(scratch),
            compiler_params=pltpu.CompilerParams(vmem_limit_bytes=VMEM_BYTES),
            cost_estimate=pl.CostEstimate(
                flops=int(self.weight * MICROSECOND), transcendentals=0, bytes_accessed=0
            ),
        )(*flat, *extra)
        return results


def swap(values, axis):
    return near(lax.ppermute(values, axis, [(0, 1), (1, 0)]))


def hop(values, bit, stride):
    size = lax.axis_size("dp")
    step = stride << bit
    return near(lax.ppermute(values, "dp", [(i, i ^ step) for i in range(size)]))


def own_bit(order, stage, stride):
    return (lax.axis_index("dp") // (stride << order[stage])) & 1


def second_kernel(order, stride, keep_ref, one_ref, send_ref):
    other = 1 - own_bit(order, 1, stride)
    total = keep_ref[other].astype(F32) + one_ref[other].astype(F32)
    send_ref[...] = total.astype(send_ref.dtype)


def third_kernel(order, stride, keep_ref, one_ref, two_ref, send_ref):
    own = own_bit(order, 1, stride)
    other = 1 - own_bit(order, 2, stride)
    total = keep_ref[own, other].astype(F32) + one_ref[own, other].astype(F32)
    send_ref[...] = (total + two_ref[other].astype(F32)).astype(send_ref.dtype)


def gathered(order, stride, keep_ref, one_ref, two_ref, three_ref):
    two, three = own_bit(order, 1, stride), own_bit(order, 2, stride)
    total = keep_ref[two, three].astype(F32) + one_ref[two, three].astype(F32)
    return total + two_ref[three].astype(F32) + three_ref[...].astype(F32)


class Chunk:
    def __init__(self, line, keep, send, order, stride):
        self.line, self.order, self.stride = line, order, stride
        self.parts = [keep, hop(send, order[0], stride)]

    def step(self):
        keep = self.parts[0]
        stage = len(self.parts) - 1
        kernel = (second_kernel, third_kernel)[stage - 1]
        (send,) = self.line.call(
            functools.partial(kernel, self.order, self.stride),
            [(keep.shape[stage:], keep.dtype)],
            *self.parts,
        )
        self.parts.append(hop(send, self.order[stage], self.stride))


def total_kernel(order, stride, parts, total_ref):
    total_ref[...] = gathered(order, stride, *parts)


def scatter_rest(line, chunk, rows):
    (total,) = line.call(
        functools.partial(total_kernel, chunk.order, chunk.stride),
        [(chunk.parts[3].shape, F32)],
        chunk.parts,
        far=1,
    )
    size, stride = lax.axis_size("dp"), chunk.stride
    groups = [[g * stride + i for i in range(stride)] for g in range(size // stride)]

    def scatter(values, dimension):
        return near(
            lax.psum_scatter(
                values, "dp", scatter_dimension=dimension, axis_index_groups=groups, tiled=True
            )
        )

    if total.shape[0] == rows:
        return [scatter(total, 0)]
    return [scatter(total[:rows], 0), scatter(total[rows : rows + 4, :rows], 1)]


def shards(
    tower_input,
    patch_order,
    visible_count,
    joint_cotangent,
    mixer_in_copy,
    mixer_in_master,
    mixer_in_moment,
    mixer_in_average,
    mixer_out_copy,
    mixer_out_master,
    mixer_out_moment,
    mixer_out_average,
    expand_copy,
    expand_master,
    expand_moment,
    expand_average,
    contract_copy,
    contract_master,
    contract_moment,
    contract_average,
    norm_params_copy,
    norm_params_master,
    norm_params_moment,
    norm_params_average,
):
    seq_count, length, width = tower_input.shape[1:]
    inner = mixer_in_copy.shape[3]
    heads = inner // HD
    hidden_width = expand_copy.shape[2]
    dp_size = lax.axis_size("dp")
    stride = dp_size // SPLIT
    tower = lax.axis_index("tower")
    line = Line()
    act = (length, width)
    both = ((seq_count,) + act, BF)
    tokens = seq_count * length
    left_scratch = pltpu.VMEM((2, width // 2, tokens), BF)
    front_outs = [
        (act, BF),
        (act, BF),
        ((3, length, inner), BF),
        ((heads, length, length), BF),
        ((length, inner), BF),
    ]
    got, chunks = {}, {}

    def lead():
        far = [
            patch_order,
            visible_count,
            tower_input[0],
            jnp.transpose(mixer_in_copy[0], (1, 0, 2)),
            norm_params_copy[0],
            mixer_out_copy[0],
            joint_cotangent.reshape(2, length, width),
        ]
        results = line.call(
            lead_kernel,
            [(v.shape, v.dtype) for v in far] + [(act, BF), (act, BF)] + front_outs,
            *far,
            raw=len(far),
            scratch=[pltpu.SemaphoreType.DMA((11,))],
        )
        got["fixed"], got["att0"], got["front0"] = results[:7], results[7], results[9:]
        got["cot_other"] = swap(results[8], "tower")
        got["att0_other"] = swap(results[7], "mp")

    def following():
        far = [expand_copy[0], contract_copy[0]]
        w_up, w_down, att, *front = line.call(
            next_kernel,
            [(v.shape, v.dtype) for v in far] + [(act, BF)] + front_outs,
            *far,
            *got["fixed"][:6],
            raw=len(far),
            scratch=[pltpu.SemaphoreType.DMA((8,))],
        )
        got["wide"], got["att1"], got["front1"] = (w_up, w_down), att, front
        got["att1_other"] = swap(att, "mp")

    mid_outs = [
        (act, F32),
        (act, BF),
        (act, BF),
        ((length, hidden_width), BF),
        ((length, hidden_width), BF),
    ]

    def mid(seq):
        _, count, _, _, norms, _, cot = got["fixed"]
        kernel, outs = (mid_kernel, []) if seq else (whole_mid_kernel, [(act, BF)] * 2)
        results = line.call(
            functools.partial(kernel, seq),
            outs + mid_outs,
            count,
            got[f"front{seq}"][0],
            got[f"att{seq}"],
            got[f"att{seq}_other"],
            norms,
            *got["wide"],
            cot,
            got["cot_other"],
        )
        if seq:
            got["mid1"] = [None, None] + results
        else:
            got["mid0"] = results
            got["back_other0"] = swap(results[0], "mp")

    def sides():
        hidden, pre = got["mid1"][5:7]
        results = line.call(sides_kernel, [(act, BF)] * 2, *got["wide"], hidden, pre)
        got["mid1"][0:2] = results
        got["back_other1"] = swap(results[0], "mp")

    def pick(name, place):
        return [got[f"{name}{seq}"][place] for seq in range(2)]

    def group(index):
        source, start, stop, order = GROUPS[index]
        cols = slice(start * hidden_width // 6, stop * hidden_width // 6)
        shape = ((2, 2, width // SPLIT, cols.stop - cols.start), BF)
        lefts, rights = ((4, 5), (3, 6))[source]
        send, left = line.call(
            functools.partial(send_kernel, order, stride, cols),
            [shape, ((width // 2, tokens), BF)],
            pick("mid", lefts),
            pick("mid", rights),
            scratch=[pltpu.VMEM((width // 2, tokens), BF)],
        )
        chunks[f"C{index}"] = Chunk(line, None, send, order, stride)
        got[f"rest{index}"] = (cols, shape, left, pick("mid", rights))

    def rest(index):
        cols, shape, left, rights = got[f"rest{index}"]
        (chunks[f"C{index}"].parts[0],) = line.call(
            functools.partial(keep_kernel, cols), [shape], left, rights
        )

    def back(seq):
        _, _, _, w_in, norms, w_out, _ = got["fixed"]
        rows, _, qkv, probs, _ = got[f"front{seq}"]
        first, _, middle, _, final, _, _ = got[f"mid{seq}"]
        got[f"last{seq}"] = line.call(
            back_kernel,
            [(act, BF), (act, BF), ((3, length, inner), BF), ((8, width), F32)],
            first,
            got[f"back_other{seq}"],
            middle,
            final,
            norms,
            w_out,
            w_in,
            qkv,
            probs,
            rows,
            got["last0"][3] if seq else None,
            scratch=[pltpu.VMEM((length, inner), BF)],
        )
        if seq:
            got["norm_other"] = swap(got["last1"][3], "mp")

    def share(name, sources):
        (result,) = line.call(copy_kernel, [both], sources)
        got[name], got[name + "_other"] = result, swap(result, "mp")

    def mixer_a():
        keep, send = line.call(
            functools.partial(mixer_a_kernel, A_ORDER, stride),
            [((2, 2, width // SPLIT + 8, 2 * inner), BF)] * 2,
            pick("front", 1),
            pick("last", 2),
            got["last1"][3],
            got["norm_other"],
            scratch=[left_scratch],
        )
        chunks["M0"] = Chunk(line, keep, send, A_ORDER, stride)

    def mixer_b():
        keep, send = line.call(
            functools.partial(mixer_b_kernel, MIX_ORDER, stride),
            [((2, 2, width // SPLIT, 2 * inner), BF)] * 2,
            pick("last", 1),
            pick("front", 4),
            pick("front", 1),
            pick("last", 2),
            scratch=[left_scratch] * 2,
        )
        chunks["M1"] = Chunk(line, keep, send, MIX_ORDER, stride)

    def fetch_masters():
        far = [
            *[jnp.transpose(v[0], (1, 0, 2)) for v in (mixer_in_master, mixer_in_moment, mixer_in_average)],
            *[v[0].T for v in (mixer_out_master, mixer_out_moment, mixer_out_average)],
            *[v[0] for v in (norm_params_master, norm_params_moment, norm_params_average)],
            *[v[0].T for v in (contract_master, contract_moment, contract_average)],
            *[v[0] for v in (expand_master, expand_moment, expand_average)],
        ]
        got["masters"] = line.call(
            fetch_kernel,
            [(v.shape, v.dtype) for v in far],
            *far,
            raw=len(far),
            scratch=[pltpu.SemaphoreType.DMA((len(far),))],
        )

    def input_side():
        patches, count, _, _, norms, _, _ = got["fixed"]
        (got["input_grad"],) = line.call(
            input_kernel,
            [both],
            patches,
            count,
            got["firsts"],
            got["firsts_other"],
            pick("front", 0),
            pick("last", 1),
            norms,
            far=1,
        )

    def final_side():
        got["keep"], send = line.call(
            final_kernel,
            [(act, BF), (act, BF)],
            got["fixed"][1],
            pick("mid", 2),
            got["outs"],
            got["outs_other"],
        )
        got["row_other"] = swap(send, "tower")

    def join():
        (got["joint"],) = line.call(
            join_kernel, [((2, length, width), BF)], got["keep"], got["row_other"], far=1
        )

    rate_scale = 1.0 / math.sqrt(seq_count * dp_size * length)

    def update(name, names, start, indices):
        lists = [[chunks[n] for n in group_names] for group_names in names]
        weights = [got["masters"][3 * i : 3 * i + 3] for i in range(start, start + len(indices))]
        sizes = [g[0].shape for g in weights]
        groups = []
        for members in lists:
            groups.append(
                [
                    (c.order, scatter_rest(line, c, width // SPLIT) if stride > 1 else c.parts)
                    for c in members
                ]
            )
        orders = [[order for order, _ in members] for members in groups]

        def kernel(parts, *refs):
            paired = [list(zip(o, p)) for o, p in zip(orders, parts)]
            update_kernel([STEP_RATES[i] * rate_scale for i in indices], stride, paired, *refs)

        values = line.call(
            kernel,
            [(s, F32 if i < 4 else BF) for s in sizes for i in range(5)],
            [[parts for _, parts in members] for members in groups],
            *[[g[i] for g in weights] for i in range(3)],
            far=5 * len(weights),
        )
        got[name] = [values[5 * i : 5 * i + 5] for i in range(len(weights))]

    def source_names(source):
        return [f"C{i}" for i, g in enumerate(GROUPS) if g[0] == source]

    steps = {
        "lead": lead,
        "next": following,
        "mid0": lambda: mid(0),
        "mid1": lambda: mid(1),
        "sides": sides,
        "back0": lambda: back(0),
        "back1": lambda: back(1),
        "cpA4": lambda: share("firsts", pick("last", 0)),
        "cpA2": lambda: share("outs", pick("mid", 1)),
        "fetch": fetch_masters,
        "kM0": mixer_a,
        "kM1": mixer_b,
        "inp": input_side,
        "fin": final_side,
        "join": join,
        "updC": lambda: update("down", [source_names(0)], 3, (3,)),
        "updE": lambda: update("up", [source_names(1)], 4, (2,)),
        "updM": lambda: update("mixer", [["M0", "M1"]], 0, (0, 1, 4)),
    }
    for name, weight in PLAN:
        line.weight = weight
        if name in steps:
            steps[name]()
        elif name.startswith("kC"):
            group(int(name[2:]))
        elif name.startswith("hC"):
            rest(int(name[2:]))
        else:
            chunks[name[2:]].step()

    in_set, out_set, norm_set = got["mixer"]
    (down_set,), (up_set,) = got["down"], got["up"]
    return (
        got["joint"].reshape(1, 1, 2, seq_count // 2, length, width),
        got["input_grad"][None],
        *[jnp.transpose(v, (1, 0, 2))[None] for v in in_set],
        *[v.T[None] for v in out_set],
        *[v[None] for v in up_set],
        *[v.T[None] for v in down_set],
        *[v[None] for v in norm_set],
    )


def solution(mesh):
    weight_in = P("tower", "dp", None, "mp")
    weight_out = P("tower", "mp", "dp")
    weight_up = P("tower", "dp", "mp")
    norm = P("tower", None, "dp")
    return jax.shard_map(
        shards,
        mesh=mesh,
        in_specs=(
            P("tower", "dp", None, None),
            P("dp", None),
            P("tower", "dp"),
            P("dp", "tower", None, None, None, None),
            P("tower", None, None, "mp"),
            *[weight_in] * 3,
            P("tower", "mp", None),
            *[weight_out] * 3,
            P("tower", None, "mp"),
            *[weight_up] * 3,
            P("tower", "mp", None),
            *[weight_out] * 3,
            P("tower", None, None),
            *[norm] * 3,
        ),
        out_specs=(
            P("dp", "tower", None, None, None, None),
            P("tower", "dp", None, None),
            *[weight_in] * 5,
            *[weight_out] * 5,
            *[weight_up] * 5,
            *[weight_out] * 5,
            *[norm] * 5,
        ),
        check_vma=False,
    )
```
